32 devices in a mesh: ctx: 16 (over z, x, core), fsdp: 2 (over y).
Axes of the slice: x: 2, y: 2, z: 4, core: 2. Of those that a mesh axis runs over, the one named last changes fastest.
Arguments:
- tokens: bfloat16 [2, 4096, 1024], P('fsdp', 'ctx'), may hold values from -6 to 6
- cotangent: bfloat16 [2, 4096, 1024], P('fsdp', 'ctx'), may hold values from -6 to 6
- w_qkv: bfloat16 [1024, 3072], P('fsdp'), may hold values from -0.25 to 0.25
- w_up: bfloat16 [1024, 4096], P('fsdp'), may hold values from -0.1875 to 0.1875
- w_out: bfloat16 [1024, 1024], P('fsdp'), may hold values from -0.375 to 0.375
- w_down: bfloat16 [4096, 1024], P('fsdp'), may hold values from -0.09375 to 0.09375
- b_qkv: bfloat16 [3072], replicated, may hold values from -0.59765625 to 0.59765625
- b_up: bfloat16 [4096], replicated, may hold values from -3 to 3
- b_out: bfloat16 [1024], replicated, may hold values from -2 to 2
- b_down: bfloat16 [1024], replicated, may hold values from -2 to 2
- ln_gain: bfloat16 [1024], replicated, may hold values from 0.5 to 1.5
- ln_bias: bfloat16 [1024], replicated, may hold values from -2 to 2
- block_table: int32 [2, 32], P('fsdp'), may hold values from 0 to 31, each once within a row
- seg_ids: int32 [2, 4096], P('fsdp'), may hold values from 0 to 2, as said below
- positions: int32 [2, 4096], P('fsdp'), may hold values from 0 to 4094, as said below
Outputs:
- output: bfloat16 [2, 4096, 1024], P('fsdp', 'ctx')
- input_grad: bfloat16 [2, 4096, 1024], P('fsdp', 'ctx')
- w_qkv_grad: float32 [1024, 3072], P('fsdp')
- w_up_grad: float32 [1024, 4096], P('fsdp')
- w_out_grad: float32 [1024, 1024], P('fsdp')
- w_down_grad: float32 [4096, 1024], P('fsdp')
- b_qkv_grad: float32 [3072], replicated
- b_up_grad: float32 [4096], replicated
- b_out_grad: float32 [1024], replicated
- b_down_grad: float32 [1024], replicated
- ln_gain_grad: float32 [1024], replicated
- ln_bias_grad: float32 [1024], replicated
The draws below stay inside these ranges and needn't reach their ends.
Inputs may be any that keep to these rules, and one draw needn't show every extreme that they name: Storage block b of group g (rows b * 128 to b * 128 + 127 along the token dimension) holds the group's logical block block_table[g, b]; each row is a permutation. `seg_ids`: in logical order, segment 0 (the prompt) is one run of 2048 tokens and each segment 1 to 2 (a continuation) one run of 1024 tokens; the runs stand in any order. `positions`: the prompt counts from 0; each continuation counts from 2048 plus an offset of its own below 1024.
All inputs are finite; a program needn't handle non-finite values.
Results may differ from the reference program's by a relative error of at most 0.015.
The reference program's roundings to bfloat16 on the way count: a program that leaves them out, or rounds other values in their place, can miss the bound.
Values may be sent and summed in bfloat16 or wider, within the bound.
A program may use at most 448 MiB of HBM per device.

```python
import math
import jax
import jax.numpy as jnp
from jax import lax

D = 1024
HEADS = 16
HDIM = 64
FF = 4096
ROT = 16
BLK = 128
CLEN = 1024
GROUPS = 2
GTOK = 4096
PROMPT = 2048
NCONT = 2
NBLK = 32


def group_layout(key):
    order_key, offset_key = jax.random.split(key)
    arrangement = jax.random.permutation(order_key, NCONT + 1)
    unit_counts = jnp.where(arrangement == 0, NCONT, 1)
    unit_starts = jnp.cumsum(unit_counts) - unit_counts
    unit_segment = jnp.repeat(arrangement, unit_counts, total_repeat_length=2 * NCONT)
    unit_first = jnp.repeat(unit_starts, unit_counts, total_repeat_length=2 * NCONT)
    token_index = jnp.arange(GTOK, dtype=jnp.int32)
    token_unit = token_index // CLEN
    segment = unit_segment[token_unit]
    within = token_index - unit_first[token_unit] * CLEN
    offsets = jax.random.randint(offset_key, (NCONT + 1,), 0, CLEN).at[1].set(CLEN - 1)
    placed = jnp.where(segment == 0, within, PROMPT + offsets[segment] + within)
    return (segment.astype(jnp.int32), placed.astype(jnp.int32))


def layout_all(key):
    group_keys = jax.random.split(jax.random.fold_in(key, 17), GROUPS)
    return jax.vmap(group_layout)(group_keys)


def draw_seg_ids(key, part):
    return layout_all(key)[0]


def draw_positions(key, part):
    return layout_all(key)[1]


def levels(stream_key, dims, pieces, low, largest):
    level, own = 1.0, jax.random.fold_in(stream_key, 6)
    for position, parts in pieces:
        heights = jnp.exp(jax.random.uniform(jax.random.fold_in(own, position), (parts,), jnp.float32, low / len(pieces), largest / len(pieces)))
        level = level * jnp.repeat(heights, dims[position] // parts).reshape([-1 if axis == position else 1 for axis in range(len(dims))])
    return level


def noise(rng, shape, scale, bound, pieces=(), kind=jnp.bfloat16):
    loudness = levels(rng, shape, pieces, -0.22, 0.18) if pieces else 1.0
    array = jax.random.normal(rng, shape, jnp.float32) * scale * loudness
    return jnp.minimum(jnp.maximum(array, -bound), bound).astype(kind)


def setup_inputs(seed: int = 0) -> dict:
    streams_of = jax.random.split(jax.random.key(seed), 16)
    return {
        "tokens": noise(streams_of[0], (GROUPS, GTOK, D), 1.0, 6.0, ((0, 2), (1, 16))),
        "cotangent": noise(streams_of[1], (GROUPS, GTOK, D), 1.0, 6.0, ((0, 2), (1, 16))),
        "w_qkv": noise(streams_of[2], (D, 3 * D), (D // 2) ** -0.5, 0.25, ((0, 2),)),
        "w_up": noise(streams_of[3], (D, FF), D ** -0.5, 0.1875, ((0, 2),)),
        "w_out": noise(streams_of[4], (D, D), (D // 4) ** -0.5, 0.375, ((0, 2),)),
        "w_down": noise(streams_of[5], (FF, D), FF ** -0.5, 0.09375, ((0, 2),)),
        "b_qkv": noise(streams_of[6], (3 * D,), 0.1, 0.59765625),
        "b_up": noise(streams_of[7], (FF,), 0.5, 3.0),
        "b_out": noise(streams_of[8], (D,), 0.3, 2.0),
        "b_down": noise(streams_of[9], (D,), 0.3, 2.0),
        "ln_gain": jnp.clip(1.0 + 0.1 * jax.random.normal(streams_of[10], (D,), jnp.float32), 0.5, 1.5).astype(jnp.bfloat16),
        "ln_bias": noise(streams_of[11], (D,), 0.3, 2.0),
        "block_table": jax.vmap(lambda own: jax.random.permutation(own, NBLK))(jax.random.split(streams_of[12], GROUPS)).reshape((GROUPS, NBLK)).astype(jnp.int32),
        "seg_ids": draw_seg_ids(jax.random.fold_in(streams_of[15], 71), 0),
        "positions": draw_positions(jax.random.fold_in(streams_of[15], 71), 0),
    }


highest = lax.Precision.HIGHEST
eps_norm = 1e-05

@jax.custom_vjp
def low(v):
    return lax.optimization_barrier(v.astype(jnp.bfloat16)).astype(jnp.float32)

@jax.custom_vjp
def low_back(v):
    return v

def low_keep(v):
    return (low(v), None)

def low_pass(kept, grad):
    return (grad,)

def back_keep(v):
    return (v, None)

def back_low(kept, grad):
    return (low(grad),)
low.defvjp(low_keep, low_pass)
low_back.defvjp(back_keep, back_low)

def layer_norm(inputs, norm_gain, norm_shift):
    centered = inputs - lax.optimization_barrier(jnp.mean(inputs, axis=-1, keepdims=True))
    variance = lax.optimization_barrier(jnp.mean(centered * centered, axis=-1, keepdims=True))
    return centered * lax.rsqrt(variance + eps_norm) * norm_gain + norm_shift

def angles_of(placed):
    frequency = 10000.0 ** (-jnp.arange(0, ROT, 2, dtype=jnp.float32) / ROT)
    phases = placed.astype(jnp.float32)[:, None, None] * frequency[None, None, :]
    return (jnp.cos(phases), jnp.sin(phases))

def rotate(values, cos_terms, sin_terms):
    halfway = ROT // 2
    first_half = values[..., :halfway]
    second_half = values[..., halfway:ROT]
    return jnp.concatenate([first_half * cos_terms - second_half * sin_terms, second_half * cos_terms + first_half * sin_terms, values[..., ROT:]], axis=-1)

def group_forward(params, inputs, logical, segment, placed):
    w_qkv, w_up, w_out, w_down, b_qkv, b_up, b_out, b_down, ln_gain, ln_bias = params
    row_count = inputs.shape[0]
    normed = low(layer_norm(inputs, ln_gain, ln_bias))
    merged_all = low_back(jnp.dot(normed, w_qkv, precision=highest) + b_qkv)
    up_proj = low_back(jnp.dot(normed, w_up, precision=highest) + b_up)
    cos_terms, sin_terms = angles_of(placed)
    queries = low(rotate(merged_all[:, :D].reshape(row_count, HEADS, HDIM), cos_terms, sin_terms))
    keys_all = low(rotate(merged_all[:, D:2 * D].reshape(row_count, HEADS, HDIM), cos_terms, sin_terms))
    values = low(merged_all[:, 2 * D:].reshape(row_count, HEADS, HDIM))
    step_rows = math.gcd(row_count, 512)
    score_scale = HDIM ** (-0.5)

    def attend_block(index):
        first_row = (index * step_rows).astype(jnp.int32)
        block_q = lax.dynamic_slice_in_dim(queries, first_row, step_rows, 0)
        block_order = lax.dynamic_slice_in_dim(logical, first_row, step_rows, 0)
        block_seg = lax.dynamic_slice_in_dim(segment, first_row, step_rows, 0)
        scores = low_back(jnp.einsum('qhd,khd->hqk', block_q, keys_all, precision=highest) * score_scale)
        allowed = (block_seg[:, None] == segment[None, :]) & (logical[None, :] <= block_order[:, None]) | (segment[None, :] == 0) & (block_seg[:, None] != 0)
        weights = jnp.where(allowed[None], jnp.exp(scores), 0.0)
        totals = lax.optimization_barrier(jnp.sum(weights, axis=-1))
        unnormed = low_back(jnp.einsum('hqk,khd->qhd', low(weights), values, precision=highest))
        return low(unnormed / jnp.transpose(totals)[:, :, None])
    attended = lax.map(jax.checkpoint(attend_block), jnp.arange(row_count // step_rows, dtype=jnp.int32))
    attended = attended.reshape(row_count, D)
    gated = low(jax.nn.gelu(up_proj, approximate=False))
    return inputs + jnp.dot(attended, w_out, precision=highest) + b_out + jnp.dot(gated, w_down, precision=highest) + b_down

def reference(tokens, cotangent, w_qkv, w_up, w_out, w_down, b_qkv, b_up, b_out, b_down, ln_gain, ln_bias, block_table, seg_ids, positions):
    token_rows = jnp.arange(GTOK, dtype=jnp.int32)
    logical = (block_table[:, token_rows // BLK] * BLK + (token_rows % BLK)[None, :]).astype(jnp.int32)
    segment = jnp.take_along_axis(seg_ids, logical, axis=1)
    placed = jnp.take_along_axis(positions, logical, axis=1)
    params = (w_qkv.astype(jnp.float32), w_up.astype(jnp.float32), w_out.astype(jnp.float32), w_down.astype(jnp.float32), b_qkv.astype(jnp.float32), b_up.astype(jnp.float32), b_out.astype(jnp.float32), b_down.astype(jnp.float32), ln_gain.astype(jnp.float32), ln_bias.astype(jnp.float32))
    inputs = tokens.astype(jnp.float32)

    def whole(layer_params, layer_inputs):

        def one_group(packed):
            return group_forward(layer_params, packed[0], packed[1], packed[2], packed[3])
        return lax.map(one_group, (layer_inputs, logical, segment, placed))
    output, pullback = jax.vjp(whole, params, inputs)
    param_grads, input_grad = pullback(cotangent.astype(jnp.float32))
    return (output.astype(jnp.bfloat16), input_grad.astype(jnp.bfloat16), param_grads[0], param_grads[1], param_grads[2], param_grads[3], param_grads[4], param_grads[5], param_grads[6], param_grads[7], param_grads[8], param_grads[9])
```

```python
import functools
import math

import jax
import jax.numpy as jnp
from jax import lax
from jax.experimental import pallas as pl
from jax.experimental.pallas import tpu as pltpu
from jax.sharding import PartitionSpec as P

D = 1024
HEADS = 16
HDIM = 64
FF = 4096
ROT = 16
CLEN = 1024
EPS = 1e-05
LANES = 128
MESH = pl.DeviceIdType.MESH
F32 = jnp.float32
BF16 = jnp.bfloat16
VMEM_SPEC = pl.BlockSpec(memory_space=pltpu.VMEM)
ANY_SPEC = pl.BlockSpec(memory_space=pl.ANY)
SCALE = HDIM**-0.5
LOG2E = math.log2(math.e)


def dot(a, b, ca=1, cb=0):
    return lax.dot_general(a, b, (((ca,), (cb,)), ((), ())), preferred_element_type=F32)


def guarded(cond, act):
    if cond is None:
        act()
    else:
        pl.when(cond)(act)


def greet(partners):
    barrier = pltpu.get_barrier_semaphore()
    for cond, device in partners:

        def signal(device=device):
            pl.semaphore_signal(barrier, inc=1, device_id=device, device_id_type=MESH)

        guarded(cond, signal)
    expected = sum(1 if cond is None else cond.astype(jnp.int32) for cond, _ in partners)
    pl.semaphore_wait(barrier, expected)


class Place:
    def __init__(self, count):
        self.depth = count // 4
        self.me = lax.axis_index("ctx")
        self.core = lax.rem(self.me, 2)
        self.x = lax.rem(lax.div(self.me, 2), 2)
        self.z = lax.div(self.me, 4)
        self.sibling = self.me + 1 - 2 * self.core
        self.across = self.me + 2 - 4 * self.x
        self.above = self.me + 4
        self.below = self.me - 4
        self.has_above = self.z < self.depth - 1
        self.has_below = self.z > 0

    def partners(self):
        return [
            (None, {"ctx": self.sibling}),
            (None, {"ctx": self.across}),
            (self.has_above, {"ctx": self.above}),
            (self.has_below, {"ctx": self.below}),
        ]

    def index(self, x, z, core):
        return (z * 2 + x) * 2 + core


def fsdp_peers(shards):
    mine = lax.axis_index("fsdp")
    return mine, [lax.rem(mine + k, shards) for k in range(1, shards)]


class Gather:
    def __init__(self, place, sources, outs, send, recv):
        self.place, self.sources, self.outs = place, sources, outs
        self.send, self.recv = send, recv
        self.started = []
        self.slot = 0

    def copies(self, shard, device, slot, own):
        for a, (source, out) in enumerate(zip(self.sources, self.outs)):
            yield pltpu.make_async_remote_copy(
                src_ref=source if own else out.at[shard],
                dst_ref=out.at[shard],
                send_sem=self.send.at[a, slot],
                recv_sem=self.recv.at[a, shard],
                device_id={"ctx": device},
                device_id_type=MESH,
            )

    def start(self, cond, shard, device, own=False):
        slot = self.slot
        self.slot += 1

        def act():
            for copy in self.copies(shard, device, slot, own):
                copy.start()

        guarded(cond, act)
        self.started.append((cond, shard, device, slot, own))

    def arrived(self, shard):
        for copy in self.copies(shard, self.place.sibling, 0, False):
            copy.wait_recv()

    def column(self, z, cond):
        shard = self.place.index(1 - self.place.x, z, self.place.core)
        guarded(cond, lambda: self.arrived(shard))
        self.start(cond, shard, self.place.sibling)

    def run(self):
        p = self.place
        own = p.me
        self.start(p.has_above, own, p.above, True)
        self.start(p.has_below, own, p.below, True)
        self.start(None, own, p.across, True)
        self.start(None, own, p.sibling, True)
        for step in range(1, p.depth):
            for sign in (1, -1):
                z = p.z - sign * step
                here = z >= 0 if sign == 1 else z < p.depth
                onward = jnp.logical_and(here, p.has_above if sign == 1 else p.has_below)
                shard = p.index(p.x, z, p.core)
                guarded(here, lambda shard=shard: self.arrived(shard))
                self.start(onward, shard, p.above if sign == 1 else p.below)
                self.start(here, shard, p.across)
                self.start(here, shard, p.sibling)
            self.columns(step - 1)
        self.columns(p.depth - 1)

    def columns(self, step):
        p = self.place
        if step == 0:
            self.column(p.z, None)
            return
        for sign in (1, -1):
            z = p.z - sign * step
            self.column(z, z >= 0 if sign == 1 else z < p.depth)

    def finish(self):
        p = self.place
        for z in range(p.depth):
            for x in range(2):
                self.arrived(p.index(x, z, 1 - p.core))
        for cond, shard, device, slot, own in self.started:

            def act(shard=shard, device=device, slot=slot, own=own):
                for copy in self.copies(shard, device, slot, own):
                    copy.wait_send()

            guarded(cond, act)


def gather_sems(count, arrays):
    depth = count // 4
    sends = 4 + 6 * (depth - 1) + 2 * depth
    return [pltpu.SemaphoreType.DMA((arrays, sends)), pltpu.SemaphoreType.DMA((arrays, count))]


def gather_kernel(count, x_ref, o_ref, send, recv, keep_sem):
    place = Place(count)
    greet(place.partners())
    keep = pltpu.make_async_copy(x_ref, o_ref.at[place.me], keep_sem)
    keep.start()
    ring = Gather(place, [x_ref], [o_ref], send, recv)
    ring.run()
    ring.finish()
    keep.wait()


def gather(x, count, collective_id):
    return pl.pallas_call(
        functools.partial(gather_kernel, count),
        out_shape=jax.ShapeDtypeStruct((count,) + x.shape, x.dtype),
        in_specs=[VMEM_SPEC],
        out_specs=ANY_SPEC,
        scratch_shapes=gather_sems(count, 1) + [pltpu.SemaphoreType.DMA],
        compiler_params=pltpu.CompilerParams(collective_id=collective_id, has_side_effects=True),
        name="gather",
    )(x)


def first_kernel(count, shards, x_ref, a_ref, b_ref, o_ref, ao_ref, bo_ref, send, recv, fsend, frecv, keep_sem):
    place = Place(count)
    mine, peers = fsdp_peers(shards)
    greet(place.partners() + [(None, {"fsdp": peer}) for peer in peers])
    keeps = [
        pltpu.make_async_copy(x_ref, o_ref.at[place.me], keep_sem.at[0]),
        pltpu.make_async_copy(a_ref, ao_ref.at[mine], keep_sem.at[1]),
        pltpu.make_async_copy(b_ref, bo_ref.at[mine], keep_sem.at[2]),
    ]
    moves = []
    for k, peer in enumerate(peers):
        for a, (source, out) in enumerate(((a_ref, ao_ref), (b_ref, bo_ref))):
            moves.append(
                pltpu.make_async_remote_copy(
                    src_ref=source,
                    dst_ref=out.at[mine],
                    send_sem=fsend.at[a, k],
                    recv_sem=frecv.at[a, k],
                    device_id={"fsdp": peer},
                    device_id_type=MESH,
                )
            )
    for move in moves + keeps:
        move.start()
    ring = Gather(place, [x_ref], [o_ref], send, recv)
    ring.run()
    ring.finish()
    for move in moves + keeps:
        move.wait()


def first_exchange(x, a, b, count, shards):
    return pl.pallas_call(
        functools.partial(first_kernel, count, shards),
        out_shape=[
            jax.ShapeDtypeStruct((count,) + x.shape, x.dtype),
            jax.ShapeDtypeStruct((shards,) + a.shape, a.dtype),
            jax.ShapeDtypeStruct((shards,) + b.shape, b.dtype),
        ],
        in_specs=[VMEM_SPEC] * 3,
        out_specs=[ANY_SPEC] * 3,
        scratch_shapes=gather_sems(count, 1)
        + [pltpu.SemaphoreType.DMA((2, shards - 1))] * 2
        + [pltpu.SemaphoreType.DMA((3,))],
        compiler_params=pltpu.CompilerParams(collective_id=0, has_side_effects=True),
        name="first_exchange",
    )(x, a, b)


def add_rows(out, terms, rows, step=32):
    def body(i, carry):
        at = pl.ds(pl.multiple_of(i * step, step), step)
        total = terms[0][at, :].astype(F32)
        for term in terms[1:]:
            total = total + term[at, :].astype(F32)
        out[at, :] = total.astype(out.dtype)
        return carry

    lax.fori_loop(0, rows // step, body, 0)


def scatter_kernel(count, p_ref, o_ref, held, pair, side, upward, downward, load, ssend, srecv, xsend, xrecv, zsend, urecv, drecv):
    place = Place(count)
    depth, rows = place.depth, o_ref.shape[0]
    greet(place.partners())

    def slot(x, z):
        return x * depth + z

    def loading(x, z):
        s = slot(x, z)
        return pltpu.make_async_copy(p_ref.at[place.index(x, z, place.core)], held.at[s], load.at[s])

    def pairing(x, z):
        s = slot(x, z)
        return pltpu.make_async_remote_copy(
            src_ref=p_ref.at[place.index(x, z, 1 - place.core)],
            dst_ref=pair.at[s],
            send_sem=ssend.at[s],
            recv_sem=srecv.at[s],
            device_id={"ctx": place.sibling},
            device_id_type=MESH,
        )

    def crossing(z):
        return pltpu.make_async_remote_copy(
            src_ref=held.at[slot(1 - place.x, z)],
            dst_ref=side.at[z],
            send_sem=xsend.at[z],
            recv_sem=xrecv.at[z],
            device_id={"ctx": place.across},
            device_id_type=MESH,
        )

    def rising(z):
        return pltpu.make_async_remote_copy(
            src_ref=held.at[slot(place.x, z)],
            dst_ref=upward.at[z],
            send_sem=zsend.at[z],
            recv_sem=urecv.at[z],
            device_id={"ctx": place.above},
            device_id_type=MESH,
        )

    def falling(z):
        return pltpu.make_async_remote_copy(
            src_ref=held.at[slot(place.x, z)],
            dst_ref=downward.at[z],
            send_sem=zsend.at[z],
            recv_sem=drecv.at[z],
            device_id={"ctx": place.below},
            device_id_type=MESH,
        )

    order = []
    for step in range(depth - 1, 0, -1):
        for sign in (1, -1):
            z = place.z + sign * step
            order.append((z, z < depth if sign == 1 else z >= 0, sign))
    order.append((place.z, None, 0))

    for z, cond, _ in order:

        def begin(z=z):
            for x in (1 - place.x, place.x):
                pairing(x, z).start()
                loading(x, z).start()

        guarded(cond, begin)

    def pair_up(z):
        for x in (1 - place.x, place.x):
            s = slot(x, z)
            loading(x, z).wait()
            pairing(x, z).wait_recv()
            add_rows(held.at[s], [held.at[s], pair.at[s]], rows)
            if x is not place.x:
                crossing(z).start()

    def pass_on(z, sign):
        mine = held.at[slot(place.x, z)]
        crossing(z).wait_recv()
        if sign == 1:

            @pl.when(place.has_below)
            def _():
                rising(z).wait_recv()
                add_rows(mine, [mine, side.at[z], upward.at[z]], rows)

            @pl.when(jnp.logical_not(place.has_below))
            def _():
                add_rows(mine, [mine, side.at[z]], rows)

            rising(z).start()
        else:

            @pl.when(place.has_above)
            def _():
                falling(z).wait_recv()
                add_rows(mine, [mine, side.at[z], downward.at[z]], rows)

            @pl.when(jnp.logical_not(place.has_above))
            def _():
                add_rows(mine, [mine, side.at[z]], rows)

            falling(z).start()

    def settle():
        z = place.z
        mine = held.at[slot(place.x, z)]
        crossing(z).wait_recv()
        inner = jnp.logical_and(place.has_below, place.has_above)

        @pl.when(place.has_below)
        def _():
            rising(z).wait_recv()

        @pl.when(place.has_above)
        def _():
            falling(z).wait_recv()

        @pl.when(inner)
        def _():
            add_rows(o_ref, [mine, side.at[z], upward.at[z], downward.at[z]], rows)

        @pl.when(jnp.logical_not(place.has_above))
        def _():
            add_rows(o_ref, [mine, side.at[z], upward.at[z]], rows)

        @pl.when(jnp.logical_not(place.has_below))
        def _():
            add_rows(o_ref, [mine, side.at[z], downward.at[z]], rows)

    for i, (z, cond, _) in enumerate(order):
        guarded(cond, lambda z=z: pair_up(z))
        if i:
            back, back_cond, back_sign = order[i - 1]
            guarded(back_cond, lambda: pass_on(back, back_sign))
    settle()

    for z, cond, sign in order:

        def end(z=z, sign=sign):
            for x in (1 - place.x, place.x):
                pairing(x, z).wait_send()
            crossing(z).wait_send()
            if sign == 1:
                rising(z).wait_send()
            elif sign == -1:
                falling(z).wait_send()

        guarded(cond, end)


def scatter(partial, count, collective_id):
    _, rows, cols = partial.shape
    depth = count // 4
    dma = pltpu.SemaphoreType.DMA
    return pl.pallas_call(
        functools.partial(scatter_kernel, count),
        out_shape=jax.ShapeDtypeStruct((rows, cols), F32),
        in_specs=[ANY_SPEC],
        out_specs=VMEM_SPEC,
        scratch_shapes=[pltpu.VMEM((2 * depth, rows, cols), BF16)] * 2
        + [pltpu.VMEM((depth, rows, cols), BF16)] * 3
        + [dma((2 * depth,))] * 3
        + [dma((depth,))] * 5,
        compiler_params=pltpu.CompilerParams(collective_id=collective_id, has_side_effects=True),
        name="scatter",
    )(partial)


def grads_kernel(count, shards, a_ref, b_ref, ao_ref, bo_ref, a_in, b_in, a_sum, b_sum, send, recv, fsend, frecv, keep_sem):
    place = Place(count)
    mine, peers = fsdp_peers(shards)
    greet(place.partners() + [(None, {"fsdp": peer}) for peer in peers])
    moves = []
    for k, peer in enumerate(peers):
        for a, (source, landing) in enumerate(((a_ref, a_in), (b_ref, b_in))):
            moves.append(
                pltpu.make_async_remote_copy(
                    src_ref=source.at[peer],
                    dst_ref=landing.at[k],
                    send_sem=fsend.at[a, k],
                    recv_sem=frecv.at[a, k],
                    device_id={"fsdp": peer},
                    device_id_type=MESH,
                )
            )
    for move in moves:
        move.start()
    for move in moves:
        move.wait_recv()
    for source, landing, total in ((a_ref, a_in, a_sum), (b_ref, b_in, b_sum)):
        terms = [source.at[mine]] + [landing.at[k] for k in range(shards - 1)]
        add_rows(total, terms, total.shape[0], 16)
    keeps = [
        pltpu.make_async_copy(a_sum, ao_ref.at[place.me], keep_sem.at[0]),
        pltpu.make_async_copy(b_sum, bo_ref.at[place.me], keep_sem.at[1]),
    ]
    for keep in keeps:
        keep.start()
    ring = Gather(place, [a_sum, b_sum], [ao_ref, bo_ref], send, recv)
    ring.run()
    ring.finish()
    for move in moves:
        move.wait_send()
    for keep in keeps:
        keep.wait()


def grads_exchange(a, b, count, shards, collective_id):
    dma = pltpu.SemaphoreType.DMA
    return pl.pallas_call(
        functools.partial(grads_kernel, count, shards),
        out_shape=[
            jax.ShapeDtypeStruct((count,) + a.shape[1:], a.dtype),
            jax.ShapeDtypeStruct((count,) + b.shape[1:], b.dtype),
        ],
        in_specs=[VMEM_SPEC] * 2,
        out_specs=[ANY_SPEC] * 2,
        scratch_shapes=[
            pltpu.VMEM((shards - 1,) + a.shape[1:], a.dtype),
            pltpu.VMEM((shards - 1,) + b.shape[1:], b.dtype),
            pltpu.VMEM(a.shape[1:], a.dtype),
            pltpu.VMEM(b.shape[1:], b.dtype),
        ]
        + gather_sems(count, 2)
        + [dma((2, shards - 1))] * 2
        + [dma((2,))],
        compiler_params=pltpu.CompilerParams(collective_id=collective_id, has_side_effects=True),
        name="grads_exchange",
    )(a, b)


def turn(values, cos, sin):
    lane = lax.broadcasted_iota(jnp.int32, values.shape, 1) % HDIM
    half = ROT // 2
    other = jnp.where(lane < half, pltpu.roll(values, LANES - half, 1), pltpu.roll(values, half, 1))
    return values * cos + other * sin


def project_kernel(x_ref, w_ref, b_ref, cos_ref, sin_ref, o_ref):
    merged = dot(x_ref[0], w_ref[...]) + b_ref[...]
    o_ref[:, :LANES] = turn(merged[:, :LANES], cos_ref[...], sin_ref[...]).astype(BF16)
    o_ref[:, LANES:] = merged[:, LANES:].astype(BF16)


def project(gathered, w, b, cos, sin):
    count, rows, _ = gathered.shape
    return pl.pallas_call(
        project_kernel,
        grid=(count,),
        out_shape=jax.ShapeDtypeStruct((count * rows, 2 * LANES), BF16),
        in_specs=[
            pl.BlockSpec((1, rows, D), lambda i: (i, 0, 0)),
            pl.BlockSpec(w.shape, lambda i: (0, 0)),
            pl.BlockSpec(b.shape, lambda i: (0, 0)),
            pl.BlockSpec((rows, LANES), lambda i: (i, 0)),
            pl.BlockSpec((rows, LANES), lambda i: (i, 0)),
        ],
        out_specs=pl.BlockSpec((rows, 2 * LANES), lambda i: (i, 0)),
        name="project",
    )(gathered, w, b, cos, sin)


TILE = 512


def below_diagonal(transposed=False):
    row = lax.broadcasted_iota(jnp.int32, (TILE, TILE), 0)
    col = lax.broadcasted_iota(jnp.int32, (TILE, TILE), 1)
    return row <= col if transposed else col <= row


def attend_kernel(tokens, block, order_ref, x_ref, o_ref, q_s, k_s, v_s):
    low = lax.broadcasted_iota(jnp.int32, (block, LANES), 1) < HDIM

    def fetch(j, carry):
        source = pl.ds(pl.multiple_of(order_ref[j] * block, block), block)
        target = pl.ds(pl.multiple_of(j * block, block), block)
        qk = x_ref[source, :LANES].astype(F32)
        q_s[target, :] = jnp.where(low, qk, 0.0).astype(BF16)
        k_s[target, :] = jnp.where(low, pltpu.roll(qk, HDIM, 1), 0.0).astype(BF16)
        v_s[target, :] = x_ref[source, LANES:]
        return carry

    lax.fori_loop(0, tokens // block, fetch, 0)
    prompt = tokens // 2
    per_run = CLEN // TILE

    def step(queries, key_tile, total, masked=False):
        at = pl.ds(pl.multiple_of(key_tile * TILE, TILE), TILE)
        weights = jnp.exp2(dot(queries, k_s[at, :], 1, 1) * (SCALE * LOG2E))
        if masked:
            weights = jnp.where(below_diagonal(), weights, 0.0)
        return total + dot(weights.astype(BF16), v_s[at, :])

    def one(tile, first, before):
        queries = q_s[pl.ds(pl.multiple_of(tile * TILE, TILE), TILE), :]
        total = step(queries, tile, jnp.zeros((TILE, LANES), F32), True)
        total = lax.fori_loop(0, before, lambda j, t: step(queries, j, t), total)
        total = lax.fori_loop(first, tile, lambda j, t: step(queries, j, t), total)
        for part in range(TILE // block):
            target = order_ref[tile * (TILE // block) + part]
            o_ref[pl.ds(pl.multiple_of(target * block, block), block), :] = total[part * block : (part + 1) * block]

    def in_prompt(tile, carry):
        one(tile, 0, 0)
        return carry

    def in_run(i, carry):
        tile = prompt // TILE + i
        one(tile, prompt // TILE + lax.div(i, per_run) * per_run, prompt // TILE)
        return carry

    lax.fori_loop(0, prompt // TILE, in_prompt, 0)
    lax.fori_loop(0, prompt // TILE, in_run, 0)


SMEM_SPEC = pl.BlockSpec(memory_space=pltpu.SMEM)


def attend(qkv, order):
    tokens = qkv.shape[0]
    block = tokens // order.shape[0]
    return pl.pallas_call(
        functools.partial(attend_kernel, tokens, block),
        out_shape=jax.ShapeDtypeStruct((tokens, LANES), F32),
        in_specs=[SMEM_SPEC, VMEM_SPEC],
        out_specs=VMEM_SPEC,
        scratch_shapes=[pltpu.VMEM((tokens, LANES), BF16)] * 3,
        name="attend",
    )(order, qkv)


def branch_kernel(
    acc_ref, x_ref, cot_ref, w_up_ref, b_up_ref, w_out_ref, keep_ref,
    out_ref, up_ref, scaled_ref, g_out_ref, g_up_ref, b_sum_ref, c_sum_ref,
):
    i = pl.program_id(0)
    units = w_up_ref.shape[1]
    acc = acc_ref[...]
    low = lax.broadcasted_iota(jnp.int32, acc.shape, 1) < HDIM
    total = jnp.where(low, pltpu.roll(acc, HDIM, 1), 1.0)
    attn = jnp.where(low, acc / total, 0.0)
    attended = (attn * keep_ref[...]).astype(BF16)
    x = x_ref[0]
    cot = cot_ref[0]
    up = dot(x, w_up_ref[...]) + b_up_ref[...]
    phi = 0.5 * (1.0 + lax.erf(up * (0.5**0.5)))
    gated = (up * phi).astype(BF16)
    slope = phi + up * jnp.exp(-0.5 * up * up) * ((2.0 * math.pi) ** -0.5)
    joined = jnp.concatenate([gated, attended], axis=1)
    out_ref[0] = dot(joined, w_out_ref[...]).astype(BF16)
    grads = dot(cot, w_out_ref[...], 1, 1)
    grad_up = (grads[:, :units] * slope).astype(BF16)
    up_ref[...] = grad_up
    grad_attn = grads[:, units:]
    scaled = jnp.where(low, grad_attn / total, 0.0)
    whole = jnp.where(low, total, 0.0)
    delta = jnp.sum(grad_attn * attn, axis=1, keepdims=True) / jnp.max(whole, axis=1, keepdims=True)
    lane = lax.broadcasted_iota(jnp.int32, acc.shape, 1)
    first = delta.astype(BF16).astype(F32)
    second = (delta - first).astype(BF16).astype(F32)
    third = delta - first - second
    scaled = jnp.where(lane == HDIM, -first, scaled)
    scaled = jnp.where(lane == HDIM + 1, -second, scaled)
    scaled = jnp.where(lane == HDIM + 2, -third, scaled)
    scaled_ref[...] = scaled.astype(BF16)
    parts = (
        (g_out_ref, dot(joined, cot, 0, 0)),
        (g_up_ref, dot(x, grad_up, 0, 0)),
        (b_sum_ref, jnp.sum(grad_up.astype(F32), axis=0, keepdims=True)),
        (c_sum_ref, jnp.sum(cot.astype(F32), axis=0, keepdims=True)),
    )

    @pl.when(i == 0)
    def _():
        for ref, value in parts:
            ref[...] = value

    @pl.when(i > 0)
    def _():
        for ref, value in parts:
            ref[...] += value


def branch(acc, gathered, cots, w_up, b_up, w_out, keep):
    count, rows, _ = gathered.shape
    tokens, units = count * rows, w_up.shape[1]
    whole = lambda shape: pl.BlockSpec(shape, lambda i: (0,) * len(shape))
    by_row = lambda cols: pl.BlockSpec((rows, cols), lambda i: (i, 0))
    by_shard = pl.BlockSpec((1, rows, D), lambda i: (i, 0, 0))
    return pl.pallas_call(
        branch_kernel,
        grid=(count,),
        out_shape=[
            jax.ShapeDtypeStruct((count, rows, D), BF16),
            jax.ShapeDtypeStruct((tokens, units), BF16),
            jax.ShapeDtypeStruct((tokens, LANES), BF16),
            jax.ShapeDtypeStruct(w_out.shape, F32),
            jax.ShapeDtypeStruct(w_up.shape, F32),
            jax.ShapeDtypeStruct((1, units), F32),
            jax.ShapeDtypeStruct((1, D), F32),
        ],
        in_specs=[
            by_row(LANES), by_shard, by_shard, whole(w_up.shape), whole(b_up.shape), whole(w_out.shape), whole(keep.shape),
        ],
        out_specs=[
            by_shard, by_row(units), by_row(LANES), whole(w_out.shape), whole(w_up.shape), whole((1, units)), whole((1, D)),
        ],
        name="branch",
    )(acc, gathered, cots, w_up, b_up, w_out, keep)


def slopes_kernel(tokens, block, order_ref, x_ref, g_ref, cos_ref, sin_ref, o_ref, q_s, k_s, r_s, v_s, g_s, dq_s):
    low = lax.broadcasted_iota(jnp.int32, (block, LANES), 1) < HDIM

    def fetch(j, carry):
        source = pl.ds(pl.multiple_of(order_ref[j] * block, block), block)
        target = pl.ds(pl.multiple_of(j * block, block), block)
        qk = x_ref[source, :LANES].astype(F32)
        rolled = pltpu.roll(qk, HDIM, 1)
        q_s[target, :] = jnp.where(low, qk, 0.0).astype(BF16)
        k_s[target, :] = jnp.where(low, rolled, 0.0).astype(BF16)
        r_s[target, :] = jnp.where(low, 0.0, rolled).astype(BF16)
        v_s[target, :] = x_ref[source, LANES:]
        g_s[target, :] = g_ref[source, :]
        dq_s[target, :] = jnp.zeros((block, LANES), F32)
        return carry

    lax.fori_loop(0, tokens // block, fetch, 0)
    prompt = tokens // 2
    per_run = CLEN // TILE

    def step(keys, values, query_tile, carry, masked=False):
        grad_k, grad_v = carry
        at = pl.ds(pl.multiple_of(query_tile * TILE, TILE), TILE)
        weights = jnp.exp2(dot(keys, q_s[at, :], 1, 1) * (SCALE * LOG2E))
        if masked:
            weights = jnp.where(below_diagonal(True), weights, 0.0)
        grads = g_s[at, :]
        slopes = (weights * dot(values, grads, 1, 1)).astype(BF16)
        grad_k = grad_k + dot(slopes, r_s[at, :])
        grad_v = grad_v + dot(weights.astype(BF16), grads)
        dq_s[at, :] += dot(slopes, keys, 0, 0)
        return grad_k, grad_v

    def one(tile, last, after):
        at = pl.ds(pl.multiple_of(tile * TILE, TILE), TILE)
        keys, values = k_s[at, :], v_s[at, :]
        zero = jnp.zeros((TILE, LANES), F32)
        carry = step(keys, values, tile, (zero, zero), True)
        carry = lax.fori_loop(tile + 1, last, lambda j, c: step(keys, values, j, c), carry)
        carry = lax.fori_loop(*after, lambda j, c: step(keys, values, j, c), carry)
        grad_k, grad_v = carry
        for part in range(TILE // block):
            target = order_ref[tile * (TILE // block) + part]
            place = pl.ds(pl.multiple_of(target * block, block), block)
            piece = slice(part * block, (part + 1) * block)
            o_ref[place, LANES:] = jnp.where(low, grad_v[piece], 0.0).astype(BF16)
        dq_s[at, :] += grad_k

    def in_prompt(tile, carry):
        one(tile, prompt // TILE, (prompt // TILE, tokens // TILE))
        return carry

    def in_run(i, carry):
        tile = prompt // TILE + i
        one(tile, prompt // TILE + (lax.div(i, per_run) + 1) * per_run, (0, 0))
        return carry

    lax.fori_loop(0, prompt // TILE, in_prompt, 0)
    lax.fori_loop(0, prompt // TILE, in_run, 0)

    def put(j, carry):
        source = pl.ds(pl.multiple_of(j * block, block), block)
        place = pl.ds(pl.multiple_of(order_ref[j] * block, block), block)
        both = dq_s[source, :] * SCALE
        o_ref[place, :LANES] = turn(both, cos_ref[place, :], -sin_ref[place, :]).astype(BF16)
        return carry

    lax.fori_loop(0, tokens // block, put, 0)


def slopes_of(qkv, scaled, order, cos, sin):
    tokens = qkv.shape[0]
    block = tokens // order.shape[0]
    return pl.pallas_call(
        functools.partial(slopes_kernel, tokens, block),
        out_shape=jax.ShapeDtypeStruct((tokens, 2 * LANES), BF16),
        in_specs=[SMEM_SPEC] + [VMEM_SPEC] * 4,
        out_specs=VMEM_SPEC,
        scratch_shapes=[pltpu.VMEM((tokens, LANES), BF16)] * 5 + [pltpu.VMEM((tokens, LANES), F32)],
        name="slopes",
    )(order, qkv, scaled, cos, sin)


def back_kernel(x_ref, g_ref, u_ref, w_ref, o_ref, gw_ref, gb_ref):
    i = pl.program_id(0)
    merged = g_ref[...]
    o_ref[0] = dot(jnp.concatenate([merged, u_ref[...]], axis=1), w_ref[...], 1, 1).astype(BF16)
    parts = (
        (gw_ref, dot(x_ref[0], merged, 0, 0)),
        (gb_ref, jnp.sum(merged.astype(F32), axis=0, keepdims=True)),
    )

    @pl.when(i == 0)
    def _():
        for ref, value in parts:
            ref[...] = value

    @pl.when(i > 0)
    def _():
        for ref, value in parts:
            ref[...] += value


def back(gathered, merged, grad_up, w_in):
    count, rows, _ = gathered.shape
    whole = lambda shape: pl.BlockSpec(shape, lambda i: (0,) * len(shape))
    by_row = lambda cols: pl.BlockSpec((rows, cols), lambda i: (i, 0))
    by_shard = pl.BlockSpec((1, rows, D), lambda i: (i, 0, 0))
    return pl.pallas_call(
        back_kernel,
        grid=(count,),
        out_shape=[
            jax.ShapeDtypeStruct((count, rows, D), BF16),
            jax.ShapeDtypeStruct((D, 2 * LANES), F32),
            jax.ShapeDtypeStruct((1, 2 * LANES), F32),
        ],
        in_specs=[by_shard, by_row(2 * LANES), by_row(grad_up.shape[1]), whole(w_in.shape)],
        out_specs=[by_shard, whole((D, 2 * LANES)), whole((1, 2 * LANES))],
        name="back",
    )(gathered, merged, grad_up, w_in)


def block_order(table, seg_ids):
    blocks = table.shape[0]
    segment = seg_ids.reshape(blocks, -1)[:, 0]
    number = jnp.arange(blocks, dtype=jnp.int32)
    stored = jnp.sum(jnp.where(table[:, None] == number[None, :], segment[None, :], 0), axis=1)
    key = stored * blocks + table
    rank = jnp.sum((key[None, :] < key[:, None]).astype(jnp.int32), axis=1)
    return jnp.sum(jnp.where(rank[None, :] == number[:, None], number[None, :], 0), axis=1)


def rotary_tables(table, positions):
    blocks = table.shape[0]
    by_block = positions.reshape(blocks, -1)
    number = jnp.arange(blocks, dtype=jnp.int32)
    pick = (table[:, None] == number[None, :])[:, :, None]
    place = jnp.sum(jnp.where(pick, by_block[None], 0), axis=1).reshape(1, -1)
    frequency = 10000.0 ** (-jnp.arange(0, ROT, 2, dtype=F32) / ROT)
    angle = frequency[:, None] * place.astype(F32)
    both = jnp.concatenate([jnp.cos(angle), jnp.sin(angle)], axis=0)
    lane = jnp.arange(LANES) % HDIM
    half = ROT // 2
    row = jnp.arange(half)
    hit = ((lane[None, :] % half) == row[:, None]) & (lane < ROT)[None, :]
    spread_cos = hit.astype(F32)
    spread_sin = jnp.where(lane < half, -1.0, 1.0)[None, :] * spread_cos
    none = jnp.zeros_like(spread_cos)
    spread = jnp.concatenate(
        [jnp.concatenate([spread_cos, none], axis=1), jnp.concatenate([none, spread_sin], axis=1)], axis=0
    )
    tables = lax.dot_general(both, spread, (((0,), (0,)), ((), ())), precision=lax.Precision.HIGHEST)
    return tables[:, :LANES] + (lane >= ROT).astype(F32)[None, :], tables[:, LANES:]


def local(
    tokens, cotangent, w_qkv, w_up, w_out, w_down, b_qkv, b_up, b_out, b_down, ln_gain, ln_bias, block_table, seg_ids, positions,
):
    shards = lax.axis_size("fsdp")
    count = lax.axis_size("ctx")
    me = lax.axis_index("ctx")
    repeat = count // HEADS
    head = me // repeat
    owned = D // shards
    part = FF // count // shards
    units = part * shards
    heads_owned = HEADS // shards

    inputs = tokens[0].astype(F32)
    rows = inputs.shape[0]
    gain = ln_gain.astype(F32)
    centered = inputs - jnp.mean(inputs, axis=-1, keepdims=True)
    rstd = lax.rsqrt(jnp.mean(centered * centered, axis=-1, keepdims=True) + EPS)
    xhat = centered * rstd
    normed = (xhat * gain + ln_bias.astype(F32)).astype(BF16)

    def columns(array, start, size):
        return lax.dynamic_slice_in_dim(array, start, size, axis=array.ndim - 1)

    def unit_columns(array):
        return [columns(array, f * (FF // shards) + part * me, part) for f in range(shards)]

    def head_columns(array):
        return [columns(array, k * D + HDIM * head, HDIM) for k in range(3)]

    pad = jnp.zeros((owned, LANES - HDIM), BF16)
    slice_in = jnp.concatenate(head_columns(w_qkv) + [pad] + unit_columns(w_up), axis=1)
    slice_out = jnp.concatenate(
        [
            lax.dynamic_slice_in_dim(w_down, part * me, part, axis=0),
            lax.dynamic_slice_in_dim(w_out, HDIM * (head % heads_owned), HDIM, axis=0),
        ],
        axis=0,
    )
    order = block_order(block_table[0], seg_ids[0])
    cos, sin = rotary_tables(block_table[0], positions[0])

    gathered, all_in, all_out = first_exchange(normed, slice_in, slice_out, count, shards)
    w_in = all_in.reshape(D, 2 * LANES + units)
    head_rows = lax.dynamic_index_in_dim(all_out[:, part:], head // heads_owned, 0, keepdims=False)
    w_rows = jnp.concatenate(
        [all_out[:, :part].reshape(units, D), head_rows, jnp.zeros((LANES - HDIM, D), BF16)], axis=0
    )
    bias = jnp.concatenate(head_columns(b_qkv.astype(F32)) + [jnp.ones((LANES - HDIM,), F32)])[None]
    unit_bias = jnp.concatenate(unit_columns(b_up.astype(F32)))[None]
    first_of_head = (me % repeat == 0) if repeat > 1 else True
    keep = jnp.where((jnp.arange(LANES) < HDIM) & first_of_head, 1.0, 0.0)[None]

    qkv = project(gathered, w_in[:, : 2 * LANES], bias, cos, sin)
    acc = attend(qkv, order)
    cots = gather(cotangent[0], count, 1)
    partial, grad_up, scaled, g_rows, g_up, g_up_bias, cot_sum = branch(
        acc, gathered, cots, w_in[:, 2 * LANES :], unit_bias, w_rows, keep
    )
    branches = scatter(partial, count, 2)
    output = (inputs + branches + b_out.astype(F32) + b_down.astype(F32)).astype(BF16)

    merged = slopes_of(qkv, scaled, order, cos, sin)
    if repeat > 1:
        merged = jnp.where(first_of_head, merged, jnp.zeros_like(merged))
    back_partial, g_qkv, g_qkv_bias = back(gathered, merged, grad_up, w_in)
    grad_normed = scatter(back_partial, count, 3)

    scaled_grad = grad_normed * gain
    mean_one = jnp.mean(scaled_grad, axis=-1, keepdims=True)
    mean_two = jnp.mean(scaled_grad * xhat, axis=-1, keepdims=True)
    grad_inputs = (scaled_grad - mean_one - xhat * mean_two) * rstd
    input_grad = (cotangent[0].astype(F32) + grad_inputs).astype(BF16)

    send_in = jnp.concatenate([g_qkv[:, :LANES], g_up], axis=1).astype(BF16).reshape(shards, owned, LANES + units)
    v_rows = owned * HDIM // D
    g_v = g_qkv[:, LANES : LANES + HDIM].reshape(shards, D // HDIM, v_rows, HDIM)
    g_v = jnp.swapaxes(g_v, 1, 2).reshape(shards, v_rows, D)
    biases = jnp.concatenate([g_qkv_bias, g_up_bias], axis=1)
    biases = jnp.concatenate([jnp.pad(biases, ((0, 0), (0, D - biases.shape[1]))), cot_sum], axis=0)
    biases_high = biases.astype(BF16)
    biases_low = (biases - biases_high.astype(F32)).astype(BF16)
    bias_rows = jnp.concatenate([biases_high, biases_low, jnp.zeros((12, D), BF16)], axis=0)
    spread = lambda array: jnp.broadcast_to(array[None], (shards,) + array.shape)
    send_out = jnp.concatenate(
        [
            g_rows[:units].reshape(shards, part, D).astype(BF16),
            spread(g_rows[units : units + HDIM].astype(BF16)),
            g_v.astype(BF16),
            spread(bias_rows),
        ],
        axis=1,
    )
    got_in, got_out = grads_exchange(send_in, send_out, count, shards, 4)

    by_head = got_in.reshape(HEADS, repeat, owned, -1)[:, 0]
    qk_grad = by_head[:, :, :LANES].reshape(HEADS, owned, 2, HDIM)
    qk_grad = jnp.transpose(qk_grad, (1, 2, 0, 3)).reshape(owned, 2 * D)
    out_by_head = got_out.reshape(HEADS, repeat, got_out.shape[1], D)[:, 0]
    at_v = part + HDIM
    v_grad = out_by_head[:, at_v : at_v + v_rows].reshape(HEADS, v_rows, D // HDIM, HDIM)
    v_grad = jnp.transpose(v_grad, (2, 1, 0, 3)).reshape(owned, D)
    w_qkv_grad = jnp.concatenate([qk_grad, v_grad], axis=1).astype(F32)
    up_grad = got_in[:, :, LANES:].reshape(count, owned, shards, part)
    w_up_grad = jnp.transpose(up_grad, (1, 2, 0, 3)).reshape(owned, FF).astype(F32)
    w_down_grad = got_out[:, :part].reshape(FF // shards, D).astype(F32)
    mine = lax.axis_index("fsdp")
    out_grad = lax.dynamic_slice_in_dim(out_by_head[:, part : part + HDIM], mine * heads_owned, heads_owned, axis=0)
    w_out_grad = out_grad.reshape(owned, D).astype(F32)

    at_bias = at_v + v_rows
    sums = got_out[:, at_bias : at_bias + 2].astype(F32) + got_out[:, at_bias + 2 : at_bias + 4].astype(F32)
    head_sums = sums[:, 0].reshape(HEADS, repeat, D)[:, 0, : 3 * HDIM].reshape(HEADS, 3, HDIM)
    b_qkv_grad = jnp.swapaxes(head_sums, 0, 1).reshape(3 * D)
    b_up_grad = jnp.transpose(
        sums[:, 0, 2 * LANES : 2 * LANES + units].reshape(count, shards, part), (1, 0, 2)
    ).reshape(FF)
    b_out_grad = sums[0, 1]
    small = lax.psum(
        jnp.stack([jnp.sum(grad_normed * xhat, axis=0), jnp.sum(grad_normed, axis=0)]), ("ctx", "fsdp")
    )
    return (
        output[None], input_grad[None], w_qkv_grad, w_up_grad, w_out_grad, w_down_grad,
        b_qkv_grad, b_up_grad, b_out_grad, b_out_grad, small[0], small[1],
    )


def solution(mesh):
    rows = P("fsdp", None)
    in_specs = (P("fsdp", "ctx", None),) * 2 + (rows,) * 4 + (P(),) * 6 + (rows,) * 3
    out_specs = (P("fsdp", "ctx", None),) * 2 + (rows,) * 4 + (P(),) * 6
    return jax.shard_map(local, mesh=mesh, in_specs=in_specs, out_specs=out_specs, check_vma=False)
```

```python
import functools
import math

import jax
import jax.numpy as jnp
from jax import lax
from jax.experimental import pallas as pl
from jax.experimental.pallas import tpu as pltpu
from jax.sharding import PartitionSpec as P
import numpy as np

D = 1024
HEADS = 16
HDIM = 64
FF = 4096
ROT = 16
CLEN = 1024
EPS = 1e-05
LANES = 128
TILE = 512
MESH = pl.DeviceIdType.MESH
F32 = jnp.float32
BF16 = jnp.bfloat16
VMEM_SPEC = pl.BlockSpec(memory_space=pltpu.VMEM)
SMEM_SPEC = pl.BlockSpec(memory_space=pltpu.SMEM)
ANY_SPEC = pl.BlockSpec(memory_space=pl.ANY)
DMA = pltpu.SemaphoreType.DMA
SCALE = HDIM**-0.5
LOG2E = math.log2(math.e)


def dot(a, b, ca=1, cb=0):
    return lax.dot_general(a, b, (((ca,), (cb,)), ((), ())), preferred_element_type=F32)


def both(*conds):
    return functools.reduce(jnp.logical_and, conds)


def when(cond, act):
    if cond is None:
        act()
    else:
        pl.when(cond)(act)


def loop(first, last, body):
    def step(i, carry):
        body(i)
        return carry

    lax.fori_loop(first, last, step, 0)


def rows_at(index, size):
    return pl.ds(pl.multiple_of(index * size, size), size)


def remote(src, dst, send, recv, device):
    return pltpu.make_async_remote_copy(
        src_ref=src, dst_ref=dst, send_sem=send, recv_sem=recv, device_id=device, device_id_type=MESH
    )


def greet(partners):
    barrier = pltpu.get_barrier_semaphore()
    for cond, device in partners:

        def signal(device=device):
            pl.semaphore_signal(barrier, inc=1, device_id=device, device_id_type=MESH)

        when(cond, signal)
    expected = sum(1 if cond is None else cond.astype(jnp.int32) for cond, _ in partners)
    pl.semaphore_wait(barrier, expected)


class Place:
    def __init__(self, count):
        self.count = count
        self.depth = count // 4
        self.me = lax.axis_index("ctx")
        self.core = lax.rem(self.me, 2)
        self.x = lax.rem(lax.div(self.me, 2), 2)
        self.z = lax.div(self.me, 4)
        self.sibling = self.me + 1 - 2 * self.core
        self.across = self.me + 2 - 4 * self.x
        self.above = self.me + 4
        self.below = self.me - 4
        self.has_above = self.z < self.depth - 1
        self.has_below = self.z > 0

    def partners(self):
        return [
            (None, {"ctx": self.sibling}),
            (None, {"ctx": self.across}),
            (self.has_above, {"ctx": self.above}),
            (self.has_below, {"ctx": self.below}),
        ]

    def index(self, x, z, core):
        return (z * 2 + x) * 2 + core

    def nth(self, k):
        z, last = self.z, self.depth - 1
        reach = jnp.minimum(z, last - z)
        half = lax.div(k + 1, 2)
        near = jnp.where(lax.rem(k, 2) == 1, z + half, z - half)
        far = jnp.where(z <= last - z, k, last - k)
        return jnp.where(k <= 2 * reach, near, far)

    def crossed(self, z, level):
        if level == 0:
            return jnp.bool_(False)
        ends = jnp.logical_or(z == 0, z == self.depth - 1)
        chosen = (ends, jnp.logical_or(ends, z == 1), z >= 0)[level - 1]
        return both(self.core == 0, chosen)


def fsdp_peers(shards):
    mine = lax.axis_index("fsdp")
    return mine, [lax.rem(mine + k, shards) for k in range(1, shards)]


class Gather:
    SENDS = 7

    def __init__(self, place, sources, outs, send, recv, level=1, wanted=()):
        self.wanted = dict(wanted)
        self.place, self.sources, self.outs, self.level = place, sources, outs, level
        self.send, self.recv = send, recv

    @staticmethod
    def sems(count, arrays):
        return [DMA((arrays, Gather.SENDS, count // 4)), DMA((arrays, count))]

    def copy(self, a, kind, k, shard, first=False):
        p = self.place
        device = (p.above, p.below, p.across, p.sibling, p.above, p.below, p.sibling)[kind]
        src = self.sources[a] if first else self.outs[a].at[shard]
        return remote(src, self.outs[a].at[shard], self.send.at[a, kind, k], self.recv.at[a, shard], {"ctx": device})

    def sends(self, k, own):
        p = self.place
        z = p.nth(k)
        cross = p.crossed(z, self.level)
        up, down = both(z <= p.z, p.has_above), both(z >= p.z, p.has_below)
        if own:
            return [(0, up), (1, down), (2, jnp.logical_or(jnp.logical_not(cross), z == p.z)), (3, None)]
        return [(4, both(cross, up)), (5, both(cross, down)), (6, None)]

    def shard(self, k, own, sibling=False):
        p = self.place
        return p.index(p.x if own else 1 - p.x, p.nth(k), 1 - p.core if sibling else p.core)

    def arrived(self, shard, arrays=None):
        for a in range(len(self.outs)) if arrays is None else arrays:
            when(self.is_wanted(a, shard), self.copy(a, 0, 0, shard).wait_recv)

    def is_wanted(self, a, shard):
        return self.wanted[a](shard) if a in self.wanted else None

    def each(self, k, own, act, first=False, arrive=False, arrays=None):
        sends = self.sends(k, own)
        shard = self.shard(k, own)
        for a in range(len(self.outs)) if arrays is None else arrays:
            if arrive:
                self.arrived(shard, [a])
            wanted = self.is_wanted(a, shard)
            for kind, cond in sends:
                cond = wanted if cond is None else cond if wanted is None else both(cond, wanted)
                when(cond, functools.partial(lambda a, kind: act(self.copy(a, kind, k, shard, first)), a, kind))

    def begin(self, arrays=None):
        self.each(0, True, lambda copy: copy.start(), first=True, arrays=arrays)

    def take(self, k):
        self.take_own(k)
        self.take_other(k - 1)

    def take_own(self, k):
        self.each(k, True, lambda copy: copy.start(), arrive=True)

    def slot(self, i):
        p, depth = self.place, self.place.depth
        middle = both(p.has_above, p.has_below)
        if i == 1:
            self.take_own(1)
        if i + 1 < depth:
            pl.when(middle)(lambda: self.take_own(i + 1))
        if i > 1:
            pl.when(jnp.logical_not(middle))(lambda: self.take_own(i))
        self.take_other(i - 1)

    def take_other(self, k):
        self.each(k, False, lambda copy: copy.start(), arrive=True)

    def take_next(self, k):
        depth = self.place.depth
        pl.when(k < depth)(lambda: self.take(k))
        pl.when(k == depth)(lambda: self.take_other(depth - 1))

    def from_sibling(self, k, own):
        self.arrived(self.shard(k, own, True))

    def finish(self):
        self.each(0, True, lambda copy: copy.wait_send(), first=True)
        loop(1, self.place.depth, lambda k: self.each(k, True, lambda copy: copy.wait_send()))
        loop(0, self.place.depth, lambda k: self.each(k, False, lambda copy: copy.wait_send()))


def add_rows(out, terms, rows, step=32, after=None):
    def body(i):
        at = rows_at(i, step)
        total = terms[0][at, :].astype(F32)
        for term in terms[1:]:
            total = total + term[at, :].astype(F32)
        out[at, :] = total.astype(out.dtype)

    loop(0, rows // step, body)


class Scatter:
    def __init__(self, place, out, mine, theirs, load, pair, side, rise, fall, ssend, srecv, xsend, xrecv, zsend, urecv, drecv, level=0):
        self.level = level
        self.p, self.out, self.mine, self.theirs, self.load = place, out, mine, theirs, load
        self.pair, self.side, self.rise, self.fall = pair, side, rise, fall
        self.ssend, self.srecv, self.xsend, self.xrecv = ssend, srecv, xsend, xrecv
        self.zsend, self.urecv, self.drecv = zsend, urecv, drecv
        self.rows = out.shape[0]
        self.columns = (1 - place.x, place.x)

    @staticmethod
    def scratch(count, rows, cols, level=0):
        depth = count // 4
        along = 2 * depth if level else depth
        buffers = [pltpu.VMEM((n, rows, cols), BF16) for n in (2 * depth, depth, along, along)]
        return buffers + [DMA((2 * depth,))] * 2 + [DMA((depth,))] * 2 + [DMA((along,))] * 3

    def crossed(self, z):
        return self.p.crossed(z, self.level)

    def z(self, k):
        return self.p.nth(self.p.depth - 1 - k)

    def slot(self, x, z):
        return x * self.p.depth + z

    def lane(self, x, z):
        return z if x is self.p.x else self.p.depth + z

    def pairing(self, x, z):
        s = self.slot(x, z)
        return remote(self.theirs(x, z), self.pair.at[s], self.ssend.at[s], self.srecv.at[s], {"ctx": self.p.sibling})

    def crossing(self, z):
        src = self.mine(1 - self.p.x, z)
        return remote(src, self.side.at[z], self.xsend.at[z], self.xrecv.at[z], {"ctx": self.p.across})

    def rising(self, x, z):
        s = self.lane(x, z)
        return remote(self.mine(x, z), self.rise.at[s], self.zsend.at[s], self.urecv.at[s], {"ctx": self.p.above})

    def falling(self, x, z):
        s = self.lane(x, z)
        return remote(self.mine(x, z), self.fall.at[s], self.zsend.at[s], self.drecv.at[s], {"ctx": self.p.below})

    def begin(self, k):
        for x in self.columns:
            self.pairing(x, self.z(k)).start()
            if self.load:
                self.load(x, self.z(k)).start()

    def pair_up(self, k):
        z = self.z(k)
        for i, x in enumerate(self.columns):
            if self.load:
                self.load(x, z).wait()
            self.pairing(x, z).wait_recv()
            mine = self.mine(x, z)
            add_rows(mine, [mine, self.pair.at[self.slot(x, z)]], self.rows)
            if i == 0:
                pl.when(jnp.logical_not(self.crossed(z)))(lambda: self.crossing(z).start())

    def along(self, x, z, extra):
        p, s, mine = self.p, self.lane(x, z), self.mine(x, z)

        def go(behind, move, landed):
            @pl.when(behind)
            def _():
                move.wait_recv()
                add_rows(mine, [mine, landed] + extra, self.rows)

            if extra:

                @pl.when(jnp.logical_not(behind))
                def _():
                    add_rows(mine, [mine] + extra, self.rows)

            move.start()

        pl.when(z > p.z)(lambda: go(p.has_below, self.rising(x, z), self.rise.at[s]))
        pl.when(z < p.z)(lambda: go(p.has_above, self.falling(x, z), self.fall.at[s]))

    def pass_on(self, k):
        z = self.z(k)
        cross = self.crossed(z)

        if self.level:

            @pl.when(cross)
            def _():
                for x in self.columns:
                    self.along(x, z, [])

        @pl.when(jnp.logical_not(cross))
        def _():
            self.crossing(z).wait_recv()
            self.along(self.p.x, z, [self.side.at[z]])

    def settle(self):
        p, z = self.p, self.p.z

        def meet(x):
            s, mine = self.lane(x, z), self.mine(x, z)

            @pl.when(p.has_below)
            def _():
                self.rising(x, z).wait_recv()
                add_rows(mine, [mine, self.rise.at[s]], self.rows)

            @pl.when(p.has_above)
            def _():
                self.falling(x, z).wait_recv()
                add_rows(mine, [mine, self.fall.at[s]], self.rows)

        if self.level:

            @pl.when(self.crossed(z))
            def _():
                meet(self.columns[0])
                self.crossing(z).start()

        meet(p.x)
        self.crossing(z).wait_recv()
        add_rows(self.out, [self.mine(p.x, z), self.side.at[z]], self.rows)

    def finish(self):
        p = self.p

        def end(k):
            z = self.z(k)
            cross = self.crossed(z)
            for x in self.columns:
                self.pairing(x, z).wait_send()
            pl.when(jnp.logical_or(jnp.logical_not(cross), z == p.z))(lambda: self.crossing(z).wait_send())
            pl.when(z != p.z)(lambda: self.rising(p.x, z).wait_send())
            if self.level:
                pl.when(both(z != p.z, cross))(lambda: self.rising(self.columns[0], z).wait_send())

        loop(0, p.depth, end)


def turn(values, trig, sign=1.0):
    lane = lax.broadcasted_iota(jnp.int32, values.shape, 1)
    rolled = pltpu.roll(trig, HDIM, 1)
    cos, sin = jnp.where(lane < HDIM, trig, rolled), jnp.where(lane < HDIM, rolled, trig)
    half = ROT // 2
    other = jnp.where(lane % HDIM < half, pltpu.roll(values, LANES - half, 1), pltpu.roll(values, half, 1))
    return values * cos + other * (sin * sign)


def norm_kernel(x_ref, gain_ref, shift_ref, o_ref):
    inputs = x_ref[...].astype(F32)
    centered = inputs - jnp.mean(inputs, axis=-1, keepdims=True)
    variance = jnp.mean(centered * centered, axis=-1, keepdims=True)
    o_ref[...] = (centered * lax.rsqrt(variance + EPS) * gain_ref[...] + shift_ref[...]).astype(BF16)


def norm(x, gain, shift):
    rows = 64
    return pl.pallas_call(
        norm_kernel,
        grid=(x.shape[0] // rows,),
        out_shape=jax.ShapeDtypeStruct(x.shape, BF16),
        in_specs=[
            pl.BlockSpec((rows, D), lambda i: (i, 0)),
            pl.BlockSpec((1, D), lambda i: (0, 0)),
            pl.BlockSpec((1, D), lambda i: (0, 0)),
        ],
        out_specs=pl.BlockSpec((rows, D), lambda i: (i, 0)),
        name="norm",
    )(x, gain, shift)


def prepare_kernel(
    count, shards, x_ref, bqkv_ref, bup_ref, gain_ref, shift_ref, bout_ref, bdown_ref, qkv_ref, up_ref, down_ref, out_ref,
    o_ref, a_ref, b_ref, bias_ref, unit_ref, gains_ref, blocks, bqkv_s, bup_s, sem,
):
    me = lax.axis_index("ctx")
    row = lambda ref: ref[...].astype(F32).reshape(1, -1)
    bqkv_s[...] = row(bqkv_ref)
    bup_s[...] = row(bup_ref)
    gains_ref[0:1, :] = row(gain_ref)
    gains_ref[1:2, :] = row(bout_ref) + row(bdown_ref)
    shift = row(shift_ref)
    part = LANES
    lanes = lambda base: pl.ds(pl.multiple_of(base, LANES), LANES)
    copies = [
        pltpu.make_async_copy(qkv_ref.at[:, lanes(k * D + lax.div(me, 2) * LANES)], blocks.at[k], sem.at[k]) for k in range(3)
    ]
    for f in range(shards):
        source = up_ref.at[:, lanes(f * (FF // shards) + part * me)]
        target = a_ref.at[:, (2 + f) * LANES : (3 + f) * LANES]
        copies.append(pltpu.make_async_copy(source, target, sem.at[3 + f]))
        unit_ref[:, f * part : (f + 1) * part] = bup_s[:, lanes(f * (FF // shards) + part * me)]
    copies.append(pltpu.make_async_copy(down_ref.at[rows_at(me, part)], b_ref.at[:part], sem.at[3 + shards]))
    source = out_ref.at[rows_at(lax.rem(me, HEADS // shards), HDIM)]
    copies.append(pltpu.make_async_copy(source, b_ref.at[part : part + HDIM], sem.at[4 + shards]))
    for copy in copies:
        copy.start()

    step = 64

    def normalize(i):
        at = rows_at(i, step)
        inputs = x_ref[at, :].astype(F32)
        centered = inputs - jnp.mean(inputs, axis=-1, keepdims=True)
        variance = jnp.mean(centered * centered, axis=-1, keepdims=True)
        o_ref[at, :] = (centered * lax.rsqrt(variance + EPS) * gains_ref[0:1, :] + shift).astype(BF16)

    loop(0, x_ref.shape[0] // step, normalize)
    even = lax.rem(me, 2) == 0

    def head_lanes(q, k, v, pad):
        low = lax.broadcasted_iota(jnp.int32, q.shape, 1) < HDIM
        swap = lambda values: pltpu.roll(values, HDIM, 1)
        qk = jnp.where(low, jnp.where(even, q, swap(q)), jnp.where(even, swap(k), k))
        return qk, jnp.where(low, jnp.where(even, v, swap(v)), pad)

    at = lambda k: lanes(k * D + lax.div(me, 2) * LANES)
    qk, v = head_lanes(*(jnp.broadcast_to(bqkv_s[:, at(k)], (8, LANES)) for k in range(3)), 1.0)
    bias_ref[:, :LANES] = qk[:1]
    bias_ref[:, LANES:] = v[:1]
    for copy in copies:
        copy.wait()

    def pick(i):
        at = rows_at(i, step)
        qk, v = head_lanes(*(blocks[k, at, :].astype(F32) for k in range(3)), 0.0)
        a_ref[at, :LANES] = qk.astype(BF16)
        a_ref[at, LANES : 2 * LANES] = v.astype(BF16)

    loop(0, a_ref.shape[0] // step, pick)


def prepare(x, vectors, w_qkv, w_up, w_down, w_out, count, shards):
    owned, units = D // shards, FF // count
    return pl.pallas_call(
        functools.partial(prepare_kernel, count, shards),
        out_shape=[
            jax.ShapeDtypeStruct(x.shape, BF16),
            jax.ShapeDtypeStruct((owned, 2 * LANES + units), BF16),
            jax.ShapeDtypeStruct((units // shards + HDIM, D), BF16),
            jax.ShapeDtypeStruct((1, 2 * LANES), F32),
            jax.ShapeDtypeStruct((1, units), F32),
            jax.ShapeDtypeStruct((2, D), F32),
        ],
        in_specs=[VMEM_SPEC] * 7 + [ANY_SPEC] * 4,
        out_specs=[VMEM_SPEC] * 6,
        scratch_shapes=[pltpu.VMEM((3, owned, LANES), BF16), pltpu.VMEM((1, 3 * D), F32), pltpu.VMEM((1, FF), F32), DMA((5 + shards,))],
        name="prepare",
    )(x, *vectors, w_qkv, w_up, w_down, w_out)


def first_kernel(
    count, shards, x_ref, a_ref, b_ref, bias_ref, pair_ref, spread_ref,
    o_ref, ao_ref, bo_ref, qkv_ref, trig_ref, land, send, recv, fsend, frecv, keep_sem, put_sem,
):
    place = Place(count)
    mine, peers = fsdp_peers(shards)
    rows, owned = x_ref.shape[0], a_ref.shape[0]
    greet(place.partners() + [(None, {"fsdp": peer}) for peer in peers])
    moves = []
    for a, (source, out) in enumerate(((a_ref, ao_ref), (b_ref, bo_ref))):
        moves.append([])
        for k, peer in enumerate(peers):
            moves[a].append(remote(source, out.at[mine], fsend.at[a, k], frecv.at[a, k], {"fsdp": peer}))
    keeps = [
        pltpu.make_async_copy(x_ref, land.at[place.me], keep_sem.at[0]),
        pltpu.make_async_copy(a_ref, ao_ref.at[mine], keep_sem.at[1]),
        pltpu.make_async_copy(b_ref, bo_ref.at[mine], keep_sem.at[2]),
    ]
    ring = Gather(place, [x_ref], [land], send, recv)
    for move in moves[0]:
        move.start()
    ring.begin()
    for move in moves[1] + keeps:
        move.start()
    for keep in keeps:
        keep.wait()

    def putting(chip):
        pair = pl.ds(chip * 2, 2)
        return pltpu.make_async_copy(land.at[pair], o_ref.at[pair], put_sem.at[chip])

    def project(chip):
        putting(chip).start()
        x = land[pl.ds(chip * 2, 2)].reshape(2 * rows, D)
        merged = bias_ref[...] + dot(x[:, :owned], ao_ref[0, :, : 2 * LANES])
        for f in range(1, shards):
            merged += dot(x[:, f * owned : (f + 1) * owned], ao_ref[f, :, : 2 * LANES])
        at = rows_at(chip, 2 * rows)
        trig = trig_ref[at, :]
        qkv_ref[at, :LANES] = turn(merged[:, :LANES], trig).astype(BF16)
        qkv_ref[at, LANES:] = merged[:, LANES:].astype(BF16)

    def tables(chip):
        at = rows_at(chip, 2 * rows)
        angles = pair_ref[:, at]
        tables = lax.dot_general(
            angles, spread_ref[:ROT, :], (((0,), (0,)), ((), ())), precision=lax.Precision.HIGHEST, preferred_element_type=F32
        )
        trig_ref[at, :] = tables + spread_ref[ROT : ROT + 1, :]

    loop(0, 2 * place.depth, tables)
    for move in moves[0]:
        move.wait_recv()

    def round_of(k):
        middle = both(place.has_above, place.has_below)
        pl.when(k == 0)(lambda: ring.take_own(1))
        pl.when(both(k + 2 < place.depth, middle))(lambda: ring.take_own(k + 2))
        pl.when(both(k > 0, k + 1 < place.depth, jnp.logical_not(middle)))(lambda: ring.take_own(k + 1))
        ring.take_other(k)
        for own in (True, False):
            ring.from_sibling(k, own)
        loop(0, 2, lambda i: project(place.nth(k) * 2 + jnp.where(i == 0, place.x, 1 - place.x)))

    loop(0, place.depth, round_of)
    ring.finish()
    for move in moves[0] + moves[1]:
        move.wait_send()
    for move in moves[1]:
        move.wait_recv()
    loop(0, 2 * place.depth, lambda chip: putting(chip).wait())


def first_stage(x, a, b, bias, pair, spread, count, shards):
    tokens = count * x.shape[0]
    return pl.pallas_call(
        functools.partial(first_kernel, count, shards),
        out_shape=[
            jax.ShapeDtypeStruct((count,) + x.shape, x.dtype),
            jax.ShapeDtypeStruct((shards,) + a.shape, a.dtype),
            jax.ShapeDtypeStruct((shards,) + b.shape, b.dtype),
            jax.ShapeDtypeStruct((tokens, 2 * LANES), BF16),
            jax.ShapeDtypeStruct((tokens, LANES), F32),
        ],
        in_specs=[VMEM_SPEC] * 6,
        out_specs=[ANY_SPEC] + [VMEM_SPEC] * 4,
        scratch_shapes=[pltpu.VMEM((count,) + x.shape, x.dtype)]
        + Gather.sems(count, 1)
        + [DMA((2, shards - 1))] * 2
        + [DMA((3,)), DMA((count // 2,))],
        compiler_params=pltpu.CompilerParams(collective_id=0, has_side_effects=True),
        name="first_stage",
    )(x, a, b, bias, pair, spread)


def diagonal(transposed=False):
    row = lax.broadcasted_iota(jnp.int32, (TILE, TILE), 0)
    col = lax.broadcasted_iota(jnp.int32, (TILE, TILE), 1)
    return row <= col if transposed else col <= row


def low_half(values):
    lane = lax.broadcasted_iota(jnp.int32, values.shape, 1)
    return jnp.where(lane < HDIM, values.astype(F32), 0.0).astype(values.dtype)


def fetch_rows(j, block, source, x_ref, pairs, swapped, values):
    target = rows_at(j, block)
    stored = x_ref[source]
    qk = stored[:, :LANES]
    pairs[target, :] = qk
    swapped[target, :] = pltpu.roll(qk.astype(F32), HDIM, 1).astype(BF16)
    values[target, :] = stored[:, LANES:]


class Attend:
    def __init__(self, tokens, pairs, swapped, values, out):
        self.prompt, self.run = tokens // 2 // TILE, CLEN // TILE
        self.pairs, self.swapped, self.values, self.out = pairs, swapped, values, out

    def tile(self, tile):
        in_prompt = tile < self.prompt
        start = self.prompt + lax.div(tile - self.prompt, self.run) * self.run
        queries = low_half(self.pairs[rows_at(tile, TILE), :])

        def step(key_tile, total, masked=False):
            at = rows_at(key_tile, TILE)
            weights = jnp.exp2(dot(queries, self.swapped[at, :], 1, 1) * (SCALE * LOG2E))
            if masked:
                weights = jnp.where(diagonal(), weights, 0.0)
            return total + dot(weights.astype(BF16), self.values[at, :])

        total = step(tile, jnp.zeros((TILE, LANES), F32), True)
        before = jnp.where(in_prompt, tile, self.prompt)
        total = lax.fori_loop(0, before, step, total)
        total = lax.fori_loop(jnp.where(in_prompt, tile, start), tile, step, total)
        parts = TILE // self.out.shape[1]
        self.out[pl.ds(tile * parts, parts)] = total.reshape(parts, -1, LANES)


def middle_kernel(
    count, shards, block, order_ref, rank_ref, qkv_ref, cot_ref, x_ref, a_ref, b_ref, bias_ref,
    part_ref, up_ref, scaled_ref, g_out_ref, g_up_ref, sums_ref, csum_ref,
    land, qk_s, kq_s, v_s, acc_s, w_s, x_s, p_s, go_s, gu_s, send, recv, keep_sem, fetch_sem, put_sem,
):
    place = Place(count)
    rows = cot_ref.shape[0]
    tokens, chip_rows = count * rows, 2 * rows
    units = a_ref.shape[1] - 2 * LANES
    part = units // shards
    greet(place.partners())
    ring = Gather(place, [cot_ref], [land], send, recv)
    ring.begin()
    keep = pltpu.make_async_copy(cot_ref, land.at[place.me], keep_sem)
    keep.start()

    attention = Attend(tokens, qk_s, kq_s, v_s, acc_s)
    loop(0, tokens // block, lambda j: fetch_rows(j, block, order_ref[j], qkv_ref, qk_s, kq_s, v_s))
    for f in range(shards):
        w_s[f * part : (f + 1) * part, :] = b_ref[f, :part, :]
    repeat = count // HEADS
    head_rows = b_ref[lax.div(lax.div(place.me, repeat), HEADS // shards), part : part + HDIM, :]
    w_s[units : units + HDIM, :] = head_rows
    w_s[units + HDIM :, :] = jnp.zeros((LANES - HDIM, D), BF16)
    go_s[...] = jnp.zeros_like(go_s)
    gu_s[...] = jnp.zeros_like(gu_s)
    sums_ref[...] = jnp.zeros_like(sums_ref)
    csum_ref[...] = jnp.zeros_like(csum_ref)

    def chip_of(t):
        return place.nth(lax.div(t, 2)) * 2 + jnp.where(lax.rem(t, 2) == 0, place.x, 1 - place.x)

    def fetching(t):
        return pltpu.make_async_copy(x_ref.at[pl.ds(chip_of(t) * 2, 2)], x_s.at[lax.rem(t, 2)], fetch_sem.at[lax.rem(t, 2)])

    def putting(t):
        return pltpu.make_async_copy(p_s.at[lax.rem(t, 2)], part_ref.at[pl.ds(chip_of(t) * 2, 2)], put_sem.at[lax.rem(t, 2)])

    split = (5 * place.depth) // 4
    fetching(0).start()
    loop(0, split, attention.tile)
    ring.take(1)
    loop(split, 2 * place.depth, attention.tile)
    keep.wait()

    low = lax.broadcasted_iota(jnp.int32, (chip_rows, LANES), 1) < HDIM
    lane = lax.broadcasted_iota(jnp.int32, (chip_rows, LANES), 1)

    def branch(t):
        chip, slot = chip_of(t), lax.rem(t, 2)
        pl.when(t + 1 < 2 * place.depth)(lambda: fetching(t + 1).start())
        pieces = [acc_s[rank_ref[chip * (chip_rows // block) + b]] for b in range(chip_rows // block)]
        acc = jnp.concatenate(pieces, axis=0)
        total = pltpu.roll(acc, HDIM, 1)
        inverse = 1.0 / jnp.where(low, total, 1.0)
        attn = jnp.where(low, acc * inverse, 0.0)
        attended = attn.astype(BF16)
        if repeat > 1:
            attended = jnp.where(lax.rem(place.me, repeat) == 0, attended, jnp.zeros_like(attended))
        fetching(t).wait()
        x = x_s[slot].reshape(chip_rows, D)
        cot = land[pl.ds(chip * 2, 2)].reshape(chip_rows, D)
        up = dot(x, a_ref[:, 2 * LANES :]) + bias_ref[...]
        phi = 0.5 * (1.0 + lax.erf(up * (0.5**0.5)))
        gated = (up * phi).astype(BF16)
        slope = phi + up * jnp.exp(-0.5 * up * up) * ((2.0 * math.pi) ** -0.5)
        joined = jnp.concatenate([gated, attended], axis=1)
        pl.when(t >= 2)(lambda: putting(t - 2).wait())
        p_s[slot] = dot(joined, w_s[...]).astype(BF16).reshape(2, rows, D)
        putting(t).start()
        grads = dot(cot, w_s[...], 1, 1)
        grad_up = (grads[:, :units] * slope).astype(BF16)
        at = rows_at(chip, chip_rows)
        up_ref[at, :] = grad_up
        grad_attn = grads[:, units:]
        scaled = jnp.where(low, grad_attn * inverse, 0.0)
        inverse_total = jnp.max(jnp.where(low, inverse, 0.0), axis=1, keepdims=True)
        delta = jnp.sum(grad_attn * attn, axis=1, keepdims=True) * inverse_total
        first = delta.astype(BF16).astype(F32)
        second = (delta - first).astype(BF16).astype(F32)
        third = delta - first - second
        scaled = jnp.where(lane == HDIM, -first, scaled)
        scaled = jnp.where(lane == HDIM + 1, -second, scaled)
        scaled = jnp.where(lane == HDIM + 2, -third, scaled)
        scaled_ref[at, :] = scaled.astype(BF16)
        go_s[...] += dot(joined, cot, 0, 0)
        gu_s[...] += dot(x, grad_up, 0, 0)
        sums_ref[...] += jnp.sum(grad_up.astype(F32), axis=0, keepdims=True)
        csum_ref[...] += jnp.sum(cot.astype(F32), axis=0, keepdims=True)

    def round_of(k):
        pl.when(k < place.depth - 1)(lambda: ring.take_next(k + 2))
        for own in (True, False):
            ring.from_sibling(k, own)
        loop(2 * k, 2 * k + 2, branch)

    loop(0, place.depth, round_of)
    g_out_ref[...] = go_s[...].astype(BF16)
    g_up_ref[...] = gu_s[...].astype(BF16)
    ring.finish()
    putting(2 * place.depth - 2).wait()
    putting(2 * place.depth - 1).wait()


def middle_stage(order, rank, qkv, cot, gathered, a, b, bias, count, shards):
    tokens = qkv.shape[0]
    rows = tokens // count
    block = tokens // order.shape[0]
    units = a.shape[1] - 2 * LANES
    width = units + LANES
    return pl.pallas_call(
        functools.partial(middle_kernel, count, shards, block),
        out_shape=[
            jax.ShapeDtypeStruct((count, rows, D), BF16),
            jax.ShapeDtypeStruct((tokens, units), BF16),
            jax.ShapeDtypeStruct((tokens, LANES), BF16),
            jax.ShapeDtypeStruct((width, D), BF16),
            jax.ShapeDtypeStruct((D, units), BF16),
            jax.ShapeDtypeStruct((1, units), F32),
            jax.ShapeDtypeStruct((1, D), F32),
        ],
        in_specs=[SMEM_SPEC] * 2 + [VMEM_SPEC] * 2 + [ANY_SPEC] + [VMEM_SPEC] * 3,
        out_specs=[ANY_SPEC] + [VMEM_SPEC] * 6,
        scratch_shapes=[
            pltpu.VMEM((count, rows, D), BF16),
            pltpu.VMEM((tokens, LANES), BF16),
            pltpu.VMEM((tokens, LANES), BF16),
            pltpu.VMEM((tokens, LANES), BF16),
            pltpu.VMEM((tokens // block, block, LANES), F32),
            pltpu.VMEM((width, D), BF16),
            pltpu.VMEM((2, 2, rows, D), BF16),
            pltpu.VMEM((2, 2, rows, D), BF16),
            pltpu.VMEM((width, D), F32),
            pltpu.VMEM((D, units), F32),
        ]
        + Gather.sems(count, 1)
        + [DMA, DMA((2,)), DMA((2,))],
        compiler_params=pltpu.CompilerParams(collective_id=1, has_side_effects=True),
        name="middle_stage",
    )(order, rank, qkv.reshape(-1, block, 2 * LANES), cot, gathered, a, b, bias)


def slopes_kernel(
    count, block, order_ref, p_ref, x_ref, g_ref, trig_ref, tok_ref, bias_ref,
    o_ref, m_ref, qk_s, kq_s, v_s, g_s, dq_s, sum_s, held, load_sem, *scratch,
):
    place = Place(count)
    depth, rows = place.depth, tok_ref.shape[0]
    tokens = count * rows
    greet(place.partners())
    slot = lambda x, z: x * depth + z
    scatter = Scatter(
        place, sum_s,
        lambda x, z: held.at[slot(x, z)],
        lambda x, z: p_ref.at[place.index(x, z, 1 - place.core)],
        lambda x, z: pltpu.make_async_copy(
            p_ref.at[place.index(x, z, place.core)], held.at[slot(x, z)], load_sem.at[slot(x, z)]
        ),
        *scratch,
    )
    scatter.begin(0)
    scatter.begin(1)

    def fetch(j):
        target = rows_at(j, block)
        fetch_rows(j, block, order_ref[j], x_ref, qk_s, kq_s, v_s)
        g_s[target, :] = g_ref[order_ref[j]]
        dq_s[target, :] = jnp.zeros((block, LANES), F32)

    loop(0, tokens // block, fetch)
    prompt, run = tokens // 2 // TILE, CLEN // TILE
    wide_low = lax.broadcasted_iota(jnp.int32, (TILE, LANES), 1) < HDIM

    def tile_of(tile):
        at = rows_at(tile, TILE)
        keys, values = low_half(kq_s[at, :]), v_s[at, :]

        def step(query_tile, carry, masked=False):
            grad_k, grad_v = carry
            at = rows_at(query_tile, TILE)
            weights = jnp.exp2(dot(keys, qk_s[at, :], 1, 1) * (SCALE * LOG2E))
            if masked:
                weights = jnp.where(diagonal(True), weights, 0.0)
            grads = g_s[at, :]
            slopes = (weights * dot(values, grads, 1, 1)).astype(BF16)
            grad_k = grad_k + dot(slopes, kq_s[at, :])
            grad_v = grad_v + dot(weights.astype(BF16), grads)
            dq_s[at, :] += dot(slopes, keys, 0, 0)
            return grad_k, grad_v

        zero = jnp.zeros((TILE, LANES), F32)
        in_prompt = tile < prompt
        end = jnp.where(in_prompt, 2 * prompt, prompt + (lax.div(tile - prompt, run) + 1) * run)
        carry = step(tile, (zero, zero), True)
        grad_k, grad_v = lax.fori_loop(tile + 1, end, step, carry)
        m_ref[at, LANES:] = jnp.where(wide_low, grad_v, 0.0).astype(BF16)
        dq_s[at, :] += jnp.where(wide_low, 0.0, grad_k)

    scatter.pair_up(0)
    tile_of(0)

    def round_of(k):
        pl.when(k + 1 < depth)(lambda: scatter.begin(k + 1))
        scatter.pair_up(k)
        scatter.pass_on(k - 1)
        tile_of(k)

    loop(1, depth, round_of)
    loop(prompt, 2 * prompt, tile_of)

    def put(j):
        at = rows_at(j, block)
        m_ref[at, :LANES] = turn(dq_s[at, :] * SCALE, trig_ref[order_ref[j]], -1.0).astype(BF16)

    loop(0, tokens // block, put)
    scatter.settle()
    step = 32

    def close(i):
        at = rows_at(i, step)
        o_ref[at, :] = (tok_ref[at, :].astype(F32) + sum_s[at, :] + bias_ref[...]).astype(BF16)

    loop(0, rows // step, close)
    scatter.finish()


def slopes_stage(order, partial, qkv, scaled, trig, tok, bias, count):
    tokens = qkv.shape[0]
    rows = tok.shape[0]
    block = tokens // order.shape[0]
    by_block = lambda array: array.reshape(-1, block, array.shape[1])
    return pl.pallas_call(
        functools.partial(slopes_kernel, count, block),
        out_shape=[jax.ShapeDtypeStruct((rows, D), BF16), jax.ShapeDtypeStruct((tokens, 2 * LANES), BF16)],
        in_specs=[SMEM_SPEC, ANY_SPEC] + [VMEM_SPEC] * 5,
        out_specs=[VMEM_SPEC] * 2,
        scratch_shapes=[pltpu.VMEM((tokens, LANES), BF16)] * 4
        + [pltpu.VMEM((tokens, LANES), F32), pltpu.VMEM((rows, D), F32), pltpu.VMEM((count // 2, rows, D), BF16), DMA((count // 2,))]
        + Scatter.scratch(count, rows, D),
        compiler_params=pltpu.CompilerParams(collective_id=2, has_side_effects=True, vmem_limit_bytes=66_000_000),
        name="slopes_stage",
    )(order, partial, by_block(qkv), by_block(scaled), by_block(trig), tok, bias)


BIAS_ROWS = 8


def last_kernel(
    count, shards, block, rank_ref, m_ref, u_ref, w_ref, x_ref, go_ref, gu_ref, us_ref, cs_ref, tok_ref, cot_ref, gain_ref,
    ig_ref, ao_ref, bo_ref, small_ref,
    x_s, parts, sum_s, gq_s, gb_s, a_src, b_src, a_in, b_in, a_sum, b_sum, v_one, v_two, v_in, v_far,
    fetch_sem, fsend, frecv, keep_sem, send, recv, vsend, vrecv, *scratch,
):
    place = Place(count)
    depth, rows = place.depth, tok_ref.shape[0]
    mine, peers = fsdp_peers(shards)
    chip_rows = 2 * rows
    owned = D // shards
    units = u_ref.shape[1]
    part = units // shards
    near = [
        {"ctx": place.z * 4 + lax.rem(place.me + i, 4), "fsdp": lax.rem(mine + k, shards)}
        for k in range(shards)
        for i in range(4)
        if i or k
    ]
    far = [{"ctx": lax.rem(place.me + 4 * i, count)} for i in range(1, depth)]
    greet([(None, device) for device in near + far])

    scatter = Scatter(
        place, sum_s,
        lambda x, z: parts.at[x * depth + z, place.core],
        lambda x, z: parts.at[x * depth + z, 1 - place.core],
        None, *scratch,
    )

    def chip_of(t):
        return scatter.z(lax.div(t, 2)) * 2 + jnp.where(lax.rem(t, 2) == 0, 1 - place.x, place.x)

    def fetching(t):
        return pltpu.make_async_copy(x_ref.at[pl.ds(chip_of(t) * 2, 2)], x_s.at[lax.rem(t, 2)], fetch_sem.at[lax.rem(t, 2)])

    fetching(0).start()
    gq_s[...] = jnp.zeros_like(gq_s)
    gb_s[...] = jnp.zeros_like(gb_s)

    def back(t):
        chip = chip_of(t)
        pl.when(t + 1 < 2 * depth)(lambda: fetching(t + 1).start())
        pieces = [m_ref[rank_ref[chip * (chip_rows // block) + b]] for b in range(chip_rows // block)]
        merged = jnp.concatenate(pieces, axis=0)
        both_grads = jnp.concatenate([merged, u_ref[rows_at(chip, chip_rows), :]], axis=1)
        where = jnp.where(lax.rem(t, 2) == 0, 1 - place.x, place.x) * depth + scatter.z(lax.div(t, 2))
        parts[where] = dot(both_grads, w_ref[...], 1, 1).astype(BF16).reshape(2, rows, D)
        fetching(t).wait()
        gq_s[...] += dot(x_s[lax.rem(t, 2)].reshape(chip_rows, D), merged, 0, 0)
        gb_s[...] += jnp.sum(merged.astype(F32), axis=0, keepdims=True)

    loop(0, 2, back)
    scatter.begin(0)

    def round_of(k):
        loop(2 * k, 2 * k + 2, back)
        scatter.begin(k)
        scatter.pair_up(k - 1)
        pl.when(k > 1)(lambda: scatter.pass_on(k - 2))

    loop(1, depth, round_of)

    at_bias = part + HDIM
    at_v = at_bias + BIAS_ROWS
    v_rows = owned * HDIM // D
    wide = jnp.concatenate([gb_s[...], us_ref[...], jnp.zeros((1, D - 2 * LANES - units), F32)], axis=1)
    row = lax.broadcasted_iota(jnp.int32, (BIAS_ROWS, D), 0)
    biases = jnp.where(row == 0, wide, jnp.where(row == 1, cs_ref[...], 0.0))
    shifted = jnp.where(row == 2, wide, jnp.where(row == 3, cs_ref[...], 0.0))
    rest = shifted - shifted.astype(BF16).astype(F32)
    bias_rows = (biases + rest).astype(BF16)
    v_low = lax.broadcasted_iota(jnp.int32, (v_rows, LANES), 1) < HDIM
    for f in range(shards):
        a_src[f, :, :LANES] = gq_s[f * owned : (f + 1) * owned, :LANES].astype(BF16)
        a_src[f, :, LANES:] = gu_ref[f * owned : (f + 1) * owned, :]
        b_src[f, :part, :] = go_ref[f * part : (f + 1) * part, :]
        b_src[f, part:at_bias, :] = go_ref[units : units + HDIM, :]
        b_src[f, at_bias:at_v, :] = bias_rows
        for m in range(D // LANES):
            top = f * owned + 2 * m * v_rows
            one = gq_s[top : top + v_rows, LANES:]
            two = pltpu.roll(gq_s[top + v_rows : top + 2 * v_rows, LANES:], HDIM, 1)
            b_src[f, at_v:, m * LANES : (m + 1) * LANES] = jnp.where(v_low, one, two).astype(BF16)

    moves = [
        remote(source.at[peer], landing.at[k], fsend.at[a, k], frecv.at[a, k], {"fsdp": peer})
        for k, peer in enumerate(peers)
        for a, (source, landing) in enumerate(((a_src, a_in), (b_src, b_in)))
    ]
    for move in moves:
        move.start()
    scatter.pair_up(depth - 1)
    scatter.pass_on(depth - 2)
    for move in moves:
        move.wait_recv()
    add_rows(a_sum, [a_src.at[mine]] + [a_in.at[k] for k in range(shards - 1)], owned)
    add_rows(b_sum, [b_src.at[mine]] + [b_in.at[k] for k in range(shards - 1)], b_sum.shape[0], 8)
    ring = Gather(place, [a_sum, b_sum], [ao_ref, bo_ref], send, recv)
    ring.begin()
    keeps = [
        pltpu.make_async_copy(a_sum, ao_ref.at[place.me], keep_sem.at[0]),
        pltpu.make_async_copy(b_sum, bo_ref.at[place.me], keep_sem.at[1]),
    ]
    for keep in keeps:
        keep.start()
    scatter.settle()

    step = 32
    v_one[...] = jnp.zeros_like(v_one)

    def close(i):
        at = rows_at(i, step)
        inputs = tok_ref[at, :].astype(F32)
        centered = inputs - jnp.mean(inputs, axis=-1, keepdims=True)
        rstd = lax.rsqrt(jnp.mean(centered * centered, axis=-1, keepdims=True) + EPS)
        xhat = centered * rstd
        grad = sum_s[at, :]
        scaled = grad * gain_ref[...]
        mean_one = jnp.mean(scaled, axis=-1, keepdims=True)
        mean_two = jnp.mean(scaled * xhat, axis=-1, keepdims=True)
        ig_ref[at, :] = (cot_ref[at, :].astype(F32) + (scaled - mean_one - xhat * mean_two) * rstd).astype(BF16)
        v_one[0:1, :] += jnp.sum(grad * xhat, axis=0, keepdims=True)
        v_one[1:2, :] += jnp.sum(grad, axis=0, keepdims=True)

    loop(0, rows // step, close)
    ones = [remote(v_one, v_in.at[i], vsend.at[i], vrecv.at[i], device) for i, device in enumerate(near)]
    for move in ones:
        move.start()
    ring.take(1)
    for move in ones:
        move.wait()
    v_two[...] = v_one[...] + sum(v_in[i] for i in range(len(near)))
    base = len(near)
    twos = [remote(v_two, v_far.at[i], vsend.at[base + i], vrecv.at[base + i], device) for i, device in enumerate(far)]
    for move in twos:
        move.start()
    loop(2, depth + 1, ring.take_next)
    for move in twos:
        move.wait()
    small_ref[...] = v_two[...] + sum(v_far[i] for i in range(len(far)))
    scatter.finish()

    def from_sibling(k):
        ring.from_sibling(k, True)
        ring.from_sibling(k, False)

    loop(0, depth, from_sibling)
    ring.finish()
    for move in moves:
        move.wait_send()
    for keep in keeps:
        keep.wait()


def last_stage(rank, merged, grad_up, w, gathered, g_out, g_up, up_sum, cot_sum, tok, cot, gain, count, shards):
    tokens, units = grad_up.shape
    rows = tok.shape[0]
    block = tokens // rank.shape[0]
    owned = D // shards
    a_shape = (owned, LANES + units)
    b_shape = (units // shards + HDIM + BIAS_ROWS + owned * HDIM // D, D)
    near, far = 4 * shards - 1, count // 4 - 1
    vmem = pltpu.VMEM
    return pl.pallas_call(
        functools.partial(last_kernel, count, shards, block),
        out_shape=[
            jax.ShapeDtypeStruct((rows, D), BF16),
            jax.ShapeDtypeStruct((count,) + a_shape, BF16),
            jax.ShapeDtypeStruct((count,) + b_shape, BF16),
            jax.ShapeDtypeStruct((2, D), F32),
        ],
        in_specs=[SMEM_SPEC] + [VMEM_SPEC] * 3 + [ANY_SPEC] + [VMEM_SPEC] * 7,
        out_specs=[VMEM_SPEC, ANY_SPEC, ANY_SPEC, VMEM_SPEC],
        scratch_shapes=[
            vmem((2, 2, rows, D), BF16),
            vmem((count // 2, 2, rows, D), BF16),
            vmem((rows, D), F32),
            vmem((D, 2 * LANES), F32),
            vmem((1, 2 * LANES), F32),
            vmem((shards,) + a_shape, BF16),
            vmem((shards,) + b_shape, BF16),
            vmem((shards - 1,) + a_shape, BF16),
            vmem((shards - 1,) + b_shape, BF16),
            vmem(a_shape, BF16),
            vmem(b_shape, BF16),
            vmem((2, D), F32),
            vmem((2, D), F32),
            vmem((near, 2, D), F32),
            vmem((far, 2, D), F32),
            DMA((2,)),
            DMA((2, shards - 1)),
            DMA((2, shards - 1)),
            DMA((2,)),
        ]
        + Gather.sems(count, 2)
        + [DMA((near + far,))] * 2
        + Scatter.scratch(count, rows, D),
        compiler_params=pltpu.CompilerParams(collective_id=3, has_side_effects=True, vmem_limit_bytes=66_000_000),
        name="last_stage",
    )(rank, merged.reshape(-1, block, 2 * LANES), grad_up, w, gathered, g_out, g_up, up_sum, cot_sum, tok, cot, gain)


class Slopes:
    def __init__(self, tokens, pairs, swapped, values, grads, dq, out):
        self.prompt, self.run = tokens // 2 // TILE, CLEN // TILE
        self.pairs, self.swapped, self.values, self.grads, self.dq, self.out = pairs, swapped, values, grads, dq, out

    def tile(self, tile):
        at = rows_at(tile, TILE)
        keys, values = low_half(self.swapped[at, :]), self.values[at, :]
        low = lax.broadcasted_iota(jnp.int32, (TILE, LANES), 1) < HDIM

        def step(query_tile, carry, masked=False):
            grad_k, grad_v = carry
            at = rows_at(query_tile, TILE)
            weights = jnp.exp2(dot(keys, self.pairs[at, :], 1, 1) * (SCALE * LOG2E))
            if masked:
                weights = jnp.where(diagonal(True), weights, 0.0)
            grads = self.grads[at, :]
            slopes = (weights * dot(values, grads, 1, 1)).astype(BF16)
            grad_k = grad_k + dot(slopes, self.swapped[at, :])
            grad_v = grad_v + dot(weights.astype(BF16), grads)
            self.dq[at, :] += dot(slopes, keys, 0, 0)
            return grad_k, grad_v

        zero = jnp.zeros((TILE, LANES), F32)
        end = jnp.where(
            tile < self.prompt, 2 * self.prompt, self.prompt + (lax.div(tile - self.prompt, self.run) + 1) * self.run
        )
        carry = step(tile, (zero, zero), True)
        grad_k, grad_v = lax.fori_loop(tile + 1, end, step, carry)
        self.out[at, LANES:] = jnp.where(low, grad_v, 0.0).astype(BF16)
        self.dq[at, :] += jnp.where(low, 0.0, grad_k)


def core_kernel(
    count, shards, block, order_ref, rank_ref, qkv_ref, cot_ref, x_ref, a_ref, b_ref, bias_ref, trig_ref, tok_ref, gains_ref,
    o_ref, m_ref, up_ref, ga_sum, gd_sum, gh_sum, sums_ref, csum_ref, land,
    cot_s, qk_s, kq_s, v_s, g_s, acc_s, dq_s, scaled_s, w_s, x_s, join_s, slope_s, go_s, gu_s, parts, sum_s,
    ga_src, gb_src, ga_in, gb_in,
    send, recv, keep_sem, fetch_sem, cot_sem, fsend, frecv, *scratch,
):
    place = Place(count)
    mine, peers = fsdp_peers(shards)
    depth, rows = place.depth, cot_ref.shape[0]
    tokens, chip_rows, chips = count * rows, 2 * rows, 2 * depth
    per_chip = chip_rows // block
    units = a_ref.shape[1] - 2 * LANES
    part, owned = units // shards, D // shards
    greet(place.partners() + [(None, {"fsdp": peer}) for peer in peers])
    ring = Gather(place, [cot_ref], [land], send, recv)
    ring.begin()
    keep = pltpu.make_async_copy(cot_ref, land.at[place.me], keep_sem)
    keep.start()
    scatter = Scatter(
        place, sum_s,
        lambda x, z: parts.at[x * depth + z, place.core],
        lambda x, z: parts.at[x * depth + z, 1 - place.core],
        None, *scratch,
    )

    def near_z(t):
        return place.nth(lax.div(t, 2))

    def near_x(t):
        return jnp.where(lax.rem(t, 2) == 0, place.x, 1 - place.x)

    def far_z(t):
        return scatter.z(lax.div(t, 2))

    def far_x(t):
        return jnp.where(lax.rem(t, 2) == 0, 1 - place.x, place.x)

    def fetching(t):
        chip = jnp.where(t < chips, far_z(t) * 2 + far_x(t), near_z(t - chips) * 2 + near_x(t - chips))
        slot = lax.rem(t, 2)
        return pltpu.make_async_copy(x_ref.at[pl.ds(chip * 2, 2)], x_s.at[slot], fetch_sem.at[slot])

    fetching(0).start()
    attention = Attend(tokens, qk_s, kq_s, v_s, acc_s)
    loop(0, tokens // block, lambda j: fetch_rows(j, block, order_ref[j], qkv_ref, qk_s, kq_s, v_s))
    for f in range(shards):
        w_s[f * part : (f + 1) * part, :] = b_ref[f, :part, :]
    w_s[units : units + HDIM, :] = b_ref[lax.div(place.me, HEADS // shards), part : part + HDIM, :]
    w_s[units + HDIM :, :] = jnp.zeros((LANES - HDIM, D), BF16)
    for ref in (go_s, gu_s, sums_ref, csum_ref, dq_s):
        ref[...] = jnp.zeros_like(ref)

    loop(0, chips - 1, attention.tile)
    ring.slot(1)
    attention.tile(chips - 1)
    keep.wait()

    low = lax.broadcasted_iota(jnp.int32, (chip_rows, LANES), 1) < HDIM
    lane = lax.broadcasted_iota(jnp.int32, (chip_rows, LANES), 1)

    def attn_of(chip):
        acc = jnp.concatenate([acc_s[rank_ref[chip * per_chip + b]] for b in range(per_chip)], axis=0)
        inverse = 1.0 / jnp.where(low, pltpu.roll(acc, HDIM, 1), 1.0)
        return jnp.where(low, acc * inverse, 0.0), inverse

    def forward(t):
        x, z = far_x(t), far_z(t)
        chip = z * 2 + x
        at = rows_at(chip, chip_rows)
        fetching(t + 1).start()
        fetching(t).wait()
        up = dot(x_s[lax.rem(t, 2)].reshape(chip_rows, D), a_ref[:, 2 * LANES :]) + bias_ref[...]
        phi = 0.5 * (1.0 + lax.erf(up * (0.5**0.5)))
        slope_s[at, :] = phi + up * jnp.exp(-0.5 * up * up) * ((2.0 * math.pi) ** -0.5)
        joined = jnp.concatenate([(up * phi).astype(BF16), attn_of(chip)[0].astype(BF16)], axis=1)
        join_s[at, :] = joined
        parts[x * depth + z] = dot(joined, w_s[...]).astype(BF16).reshape(2, rows, D)

    def backward(t):
        chip = near_z(t) * 2 + near_x(t)
        at = rows_at(chip, chip_rows)
        pl.when(t + 1 < chips)(lambda: fetching(chips + t + 1).start())
        attn, inverse = attn_of(chip)
        cot_fetching(t).wait()
        cot = cot_s[lax.rem(t, 2)].reshape(chip_rows, D)
        grads = dot(cot, w_s[...], 1, 1)
        grad_up = (grads[:, :units] * slope_s[at, :]).astype(BF16)
        up_ref[at, :] = grad_up
        grad_attn = grads[:, units:]
        scaled = jnp.where(low, grad_attn * inverse, 0.0)
        inverse_total = jnp.max(jnp.where(low, inverse, 0.0), axis=1, keepdims=True)
        delta = jnp.sum(grad_attn * attn, axis=1, keepdims=True) * inverse_total
        first = delta.astype(BF16).astype(F32)
        second = (delta - first).astype(BF16).astype(F32)
        third = delta - first - second
        scaled = jnp.where(lane == HDIM, -first, scaled)
        scaled = jnp.where(lane == HDIM + 1, -second, scaled)
        scaled = jnp.where(lane == HDIM + 2, -third, scaled).astype(BF16)
        scaled_s[pl.ds(chip * per_chip, per_chip)] = scaled.reshape(per_chip, block, LANES)
        go_s[...] += dot(join_s[at, :], cot, 0, 0)
        fetching(chips + t).wait()
        gu_s[...] += dot(grad_up, x_s[lax.rem(t, 2)].reshape(chip_rows, D), 0, 0)
        sums_ref[...] += jnp.sum(grad_up.astype(F32), axis=0, keepdims=True)
        csum_ref[...] += jnp.sum(cot.astype(F32), axis=0, keepdims=True)

    def cot_fetching(t):
        chip, slot = near_z(t) * 2 + near_x(t), lax.rem(t, 2)
        return pltpu.make_async_copy(land.at[pl.ds(chip * 2, 2)], cot_s.at[slot], cot_sem.at[slot])

    def forward_round(k):
        loop(2 * k, 2 * k + 2, forward)
        scatter.begin(k)

    loop(0, 2, forward_round)
    ring.slot(2)
    loop(2, depth, forward_round)
    ring.slot(3)
    scatter.pair_up(0)
    scatter.pair_up(1)
    lag = jnp.where(both(place.has_above, place.has_below), 2, 0)

    def pass_on(k):
        turn_k = k - lag
        pl.when(both(turn_k >= 0, turn_k < depth - 1))(lambda: scatter.pass_on(turn_k))

    def backward_round(k):
        pl.when(k == depth - 1)(lambda: ring.take_other(depth - 1))
        for own in (True, False):
            ring.from_sibling(k, own)
        for i in range(2):
            cot_fetching(2 * k + i).start()
        loop(2 * k, 2 * k + 2, backward)

    loop(0, depth, backward_round)
    loop(2, depth, scatter.pair_up)

    ga_src[...] = gu_s[...].T.astype(BF16)
    gb_src[...] = go_s[...].astype(BF16)
    moves = []
    for k, peer in enumerate(peers):
        for a, (source, landing) in enumerate(
            (
                (ga_src.at[rows_at(peer, owned)], ga_in.at[k]),
                (gb_src.at[rows_at(peer, part)], gb_in.at[k, :part]),
                (gb_src.at[units : units + HDIM], gb_in.at[k, part:]),
            )
        ):
            moves.append(remote(source, landing, fsend.at[a, k], frecv.at[a, k], {"fsdp": peer}))
    for move in moves:
        move.start()

    def fetch_grads(j):
        g_s[rows_at(j, block), :] = scaled_s[order_ref[j]]

    loop(0, tokens // block, fetch_grads)
    slopes = Slopes(tokens, qk_s, kq_s, v_s, g_s, dq_s, m_ref)
    pass_on(0)
    slopes.tile(0)
    pass_on(1)
    slopes.tile(1)
    pass_on(2)

    def tile_round(k):
        slopes.tile(k)
        pass_on(k + 1)

    loop(2, depth, tile_round)
    loop(depth, chips, slopes.tile)

    def put(j):
        at = rows_at(j, block)
        m_ref[at, :LANES] = turn(dq_s[at, :] * SCALE, trig_ref[order_ref[j]], -1.0).astype(BF16)

    loop(0, tokens // block, put)
    out_bias = gains_ref[1:2, :]
    for move in moves:
        move.wait_recv()
    add_rows(ga_sum, [ga_src.at[rows_at(mine, owned)]] + [ga_in.at[k] for k in range(shards - 1)], owned)
    add_rows(gd_sum, [gb_src.at[rows_at(mine, part)]] + [gb_in.at[k, :part] for k in range(shards - 1)], part)
    add_rows(gh_sum, [gb_src.at[units : units + HDIM]] + [gb_in.at[k, part:] for k in range(shards - 1)], HDIM)
    scatter.settle()
    step = 32

    def close(i):
        at = rows_at(i, step)
        o_ref[at, :] = (tok_ref[at, :].astype(F32) + sum_s[at, :] + out_bias).astype(BF16)

    loop(0, rows // step, close)
    ring.finish()
    scatter.finish()

    for move in moves:
        move.wait_send()


def core_stage(order, rank, qkv, cot, gathered, a, b, bias, trig, tok, gains, count, shards):
    tokens = qkv.shape[0]
    rows = tokens // count
    blocks = order.shape[0]
    block = tokens // blocks
    units = a.shape[1] - 2 * LANES
    width, part, owned = units + LANES, units // shards, D // shards
    by_block = lambda array: array.reshape(blocks, block, array.shape[1])
    vmem = pltpu.VMEM
    ga, gb = (owned, units), (part + HDIM, D)
    return pl.pallas_call(
        functools.partial(core_kernel, count, shards, block),
        out_shape=[
            jax.ShapeDtypeStruct((rows, D), BF16),
            jax.ShapeDtypeStruct((tokens, 2 * LANES), BF16),
            jax.ShapeDtypeStruct((tokens, units), BF16),
            jax.ShapeDtypeStruct(ga, BF16),
            jax.ShapeDtypeStruct((part, D), BF16),
            jax.ShapeDtypeStruct((HDIM, D), BF16),
            jax.ShapeDtypeStruct((1, units), F32),
            jax.ShapeDtypeStruct((1, D), F32),
            jax.ShapeDtypeStruct((count, rows, D), BF16),
        ],
        in_specs=[SMEM_SPEC] * 2 + [VMEM_SPEC] * 2 + [ANY_SPEC] + [VMEM_SPEC] * 6,
        out_specs=[VMEM_SPEC] * 8 + [ANY_SPEC],
        scratch_shapes=[vmem((2, 2, rows, D), BF16)]
        + [vmem((tokens, LANES), BF16)] * 4
        + [
            vmem((blocks, block, LANES), F32),
            vmem((tokens, LANES), F32),
            vmem((blocks, block, LANES), BF16),
            vmem((width, D), BF16),
            vmem((2, 2, rows, D), BF16),
            vmem((tokens, width), BF16),
            vmem((tokens, units), F32),
            vmem((width, D), F32),
            vmem((units, D), F32),
            vmem((count // 2, 2, rows, D), BF16),
            vmem((rows, D), F32),
            vmem((D, units), BF16),
            vmem((width, D), BF16),
            vmem((shards - 1,) + ga, BF16),
            vmem((shards - 1,) + gb, BF16),
        ]
        + Gather.sems(count, 1)
        + [DMA, DMA((2,)), DMA((2,))]
        + [DMA((3, shards - 1))] * 2
        + Scatter.scratch(count, rows, D),
        compiler_params=pltpu.CompilerParams(collective_id=4, has_side_effects=True, vmem_limit_bytes=66_000_000),
        name="core_stage",
    )(order, rank, by_block(qkv), cot, gathered, a, b, bias, by_block(trig), tok, gains)


def end_kernel(
    count, shards, block, rank_ref, m_ref, u_ref, w_ref, x_ref, ga_ref, gd_ref, gh_ref, us_ref, cs_ref, tok_ref, cot_ref, gains_ref,
    ig_ref, gao_ref, gdo_ref, gho_ref, ao_ref, bo_ref, small_ref,
    x_s, parts, sum_s, gq_s, gb_s, a_src, b_src, a_in, b_in, a_sum, b_sum, v_one, v_in,
    fetch_sem, fsend, frecv, keep_sem, send, recv, vsend, vrecv, *scratch,
):
    place = Place(count)
    depth, rows = place.depth, tok_ref.shape[0]
    mine, peers = fsdp_peers(shards)
    chip_rows, chips = 2 * rows, 2 * depth
    per_chip = chip_rows // block
    owned, units = D // shards, u_ref.shape[1]
    everyone = [
        {"ctx": lax.rem(place.me + i, count), "fsdp": lax.rem(mine + k, shards)}
        for k in range(shards)
        for i in range(count)
        if i or k
    ]
    greet([(None, device) for device in everyone])
    sources, outs = [ga_ref, gd_ref, gh_ref, a_sum, b_sum], [gao_ref, gdo_ref, gho_ref, ao_ref, bo_ref]
    owns_head = lambda shard: lax.div(shard, HEADS // shards) == mine
    ring = Gather(place, sources, outs, send, recv, wanted={2: owns_head})
    keeps = [
        pltpu.make_async_copy(source, out.at[place.me], keep_sem.at[a])
        for a, (source, out) in enumerate(zip(ring.sources, ring.outs))
    ]
    ring.begin([0, 1, 2])
    for keep in keeps[:3]:
        keep.start()
    scatter = Scatter(
        place, sum_s,
        lambda x, z: parts.at[x * depth + z, place.core],
        lambda x, z: parts.at[x * depth + z, 1 - place.core],
        None, *scratch, level=1,
    )

    def far_x(t):
        return jnp.where(lax.rem(t, 2) == 0, 1 - place.x, place.x)

    def far_z(t):
        return scatter.z(lax.div(t, 2))

    def fetching(t):
        slot = lax.rem(t, 2)
        return pltpu.make_async_copy(x_ref.at[pl.ds((far_z(t) * 2 + far_x(t)) * 2, 2)], x_s.at[slot], fetch_sem.at[slot])

    fetching(0).start()
    gq_s[...] = jnp.zeros_like(gq_s)
    gb_s[...] = jnp.zeros_like(gb_s)

    def back(t):
        x, z = far_x(t), far_z(t)
        chip = z * 2 + x
        pl.when(t + 1 < chips)(lambda: fetching(t + 1).start())
        merged = jnp.concatenate([m_ref[rank_ref[chip * per_chip + b]] for b in range(per_chip)], axis=0)
        joined = jnp.concatenate([merged, u_ref[rows_at(chip, chip_rows), :]], axis=1)
        parts[x * depth + z] = dot(joined, w_ref[...], 1, 1).astype(BF16).reshape(2, rows, D)
        fetching(t).wait()
        gq_s[...] += dot(merged, x_s[lax.rem(t, 2)].reshape(chip_rows, D), 0, 0)
        gb_s[...] += jnp.sum(merged.astype(F32), axis=0, keepdims=True)

    def back_round(k):
        loop(2 * k, 2 * k + 2, back)
        scatter.begin(k)
        pl.when(k > 0)(lambda: scatter.pair_up(k - 1))

    loop(0, depth, back_round)
    scatter.pair_up(depth - 1)

    v_rows = owned * HDIM // D
    wide = jnp.concatenate([gb_s[...], us_ref[...], jnp.zeros((1, D - 2 * LANES - units), F32)], axis=1)
    row = lax.broadcasted_iota(jnp.int32, (BIAS_ROWS, D), 0)
    biases = jnp.where(row == 0, wide, jnp.where(row == 1, cs_ref[...], 0.0))
    shifted = jnp.where(row == 2, wide, jnp.where(row == 3, cs_ref[...], 0.0))
    rest = shifted - shifted.astype(BF16).astype(F32)
    bias_rows = (biases + rest).astype(BF16)
    low = lax.broadcasted_iota(jnp.int32, (v_rows, LANES), 1) < HDIM
    for f in range(shards):
        grads = gq_s[:, f * owned : (f + 1) * owned].T
        a_src[f] = grads[:, :LANES].astype(BF16)
        b_src[f, :BIAS_ROWS, :] = bias_rows
        for m in range(D // LANES):
            top = 2 * m * v_rows
            one = grads[top : top + v_rows, LANES:]
            two = pltpu.roll(grads[top + v_rows : top + 2 * v_rows, LANES:], HDIM, 1)
            b_src[f, BIAS_ROWS:, m * LANES : (m + 1) * LANES] = jnp.where(low, one, two).astype(BF16)

    moves = [
        remote(source.at[peer], landing.at[k], fsend.at[a, k], frecv.at[a, k], {"fsdp": peer})
        for k, peer in enumerate(peers)
        for a, (source, landing) in enumerate(((a_src, a_in), (b_src, b_in)))
    ]
    for move in moves:
        move.start()
    lag = jnp.where(both(place.has_above, place.has_below), 1, 0)

    def pass_on(k):
        turn_k = k - lag
        pl.when(both(turn_k >= 0, turn_k < depth - 1))(lambda: scatter.pass_on(turn_k))

    pass_on(0)
    pass_on(1)
    for move in moves:
        move.wait_recv()
    add_rows(a_sum, [a_src.at[mine]] + [a_in.at[k] for k in range(shards - 1)], owned)
    add_rows(b_sum, [b_src.at[mine]] + [b_in.at[k] for k in range(shards - 1)], b_sum.shape[0], 8)
    ring.begin([3, 4])
    for keep in keeps[3:]:
        keep.start()

    loop(2, depth, pass_on)
    ring.take_own(1)
    middle = both(place.has_above, place.has_below)
    pl.when(middle)(lambda: ring.take_own(2))
    scatter.settle()

    step = 32
    v_one[...] = jnp.zeros_like(v_one)

    def close(i):
        at = rows_at(i, step)
        inputs = tok_ref[at, :].astype(F32)
        centered = inputs - jnp.mean(inputs, axis=-1, keepdims=True)
        rstd = lax.rsqrt(jnp.mean(centered * centered, axis=-1, keepdims=True) + EPS)
        xhat = centered * rstd
        grad = sum_s[at, :]
        scaled = grad * gains_ref[0:1, :]
        mean_one = jnp.mean(scaled, axis=-1, keepdims=True)
        mean_two = jnp.mean(scaled * xhat, axis=-1, keepdims=True)
        ig_ref[at, :] = (cot_ref[at, :].astype(F32) + (scaled - mean_one - xhat * mean_two) * rstd).astype(BF16)
        v_one[0:1, :] += jnp.sum(grad * xhat, axis=0, keepdims=True)
        v_one[1:2, :] += jnp.sum(grad, axis=0, keepdims=True)

    loop(0, rows // step, close)
    ones = [remote(v_one, v_in.at[i], vsend.at[i], vrecv.at[i], device) for i, device in enumerate(everyone)]
    for move in ones:
        move.start()
    ring.take_other(0)
    pl.when(jnp.logical_not(middle))(lambda: ring.take_own(2))
    ring.take_other(1)
    loop(3, depth + 1, ring.take_next)
    scatter.finish()

    def from_sibling(k):
        ring.from_sibling(k, True)
        ring.from_sibling(k, False)

    loop(0, depth, from_sibling)
    ring.finish()
    for move in ones:
        move.wait()
    small_ref[...] = v_one[...] + sum(v_in[i] for i in range(len(everyone)))
    for move in moves:
        move.wait_send()
    for keep in keeps:
        keep.wait()


def end_stage(rank, merged, grad_up, w, gathered, g_up, g_down, g_head, up_sum, cot_sum, tok, cot, gains, count, shards):
    tokens, units = grad_up.shape
    rows = tok.shape[0]
    block = tokens // rank.shape[0]
    owned = D // shards
    a_shape = (owned, LANES)
    b_shape = (BIAS_ROWS + owned * HDIM // D, D)
    others = count * shards - 1
    vmem = pltpu.VMEM
    return pl.pallas_call(
        functools.partial(end_kernel, count, shards, block),
        out_shape=[
            jax.ShapeDtypeStruct((rows, D), BF16),
            jax.ShapeDtypeStruct((count,) + g_up.shape, BF16),
            jax.ShapeDtypeStruct((count,) + g_down.shape, BF16),
            jax.ShapeDtypeStruct((count,) + g_head.shape, BF16),
            jax.ShapeDtypeStruct((count,) + a_shape, BF16),
            jax.ShapeDtypeStruct((count,) + b_shape, BF16),
            jax.ShapeDtypeStruct((2, D), F32),
        ],
        in_specs=[SMEM_SPEC] + [VMEM_SPEC] * 3 + [ANY_SPEC] + [VMEM_SPEC] * 8,
        out_specs=[VMEM_SPEC] + [ANY_SPEC] * 5 + [VMEM_SPEC],
        scratch_shapes=[
            vmem((2, 2, rows, D), BF16),
            vmem((count // 2, 2, rows, D), BF16),
            vmem((rows, D), F32),
            vmem((2 * LANES, D), F32),
            vmem((1, 2 * LANES), F32),
            vmem((shards,) + a_shape, BF16),
            vmem((shards,) + b_shape, BF16),
            vmem((shards - 1,) + a_shape, BF16),
            vmem((shards - 1,) + b_shape, BF16),
            vmem(a_shape, BF16),
            vmem(b_shape, BF16),
            vmem((2, D), F32),
            vmem((others, 2, D), F32),
            DMA((2,)),
            DMA((2, shards - 1)),
            DMA((2, shards - 1)),
            DMA((5,)),
        ]
        + Gather.sems(count, 5)
        + [DMA((others,))] * 2
        + Scatter.scratch(count, rows, D, 1),
        compiler_params=pltpu.CompilerParams(collective_id=5, has_side_effects=True, vmem_limit_bytes=66_000_000),
        name="end_stage",
    )(rank, merged.reshape(-1, block, 2 * LANES), grad_up, w, gathered, g_up, g_down, g_head, up_sum, cot_sum, tok, cot, gains)


def place_kernel(first_ref, up_in, rows_in, qk_in, v_in, head_in, qkv_ref, up_ref, down_ref, out_ref, qkv_s, up_s, sem):
    j, steps = pl.program_id(0), pl.num_programs(0)
    slot = lax.rem(j, 2)
    owned = qk_in.shape[1]
    shards = up_in.shape[2] // LANES
    v_rows = v_in.shape[1] - BIAS_ROWS
    low = lax.broadcasted_iota(jnp.int32, (owned, LANES), 1) < HDIM
    v_low = low[:v_rows]

    def copies(j):
        slot = lax.rem(j, 2)
        for t in range(3):
            at = pl.ds(pl.multiple_of(t * D + j * LANES, LANES), LANES)
            yield pltpu.make_async_copy(qkv_s.at[slot, t], qkv_ref.at[:, at], sem.at[slot, t])
        for f in range(shards):
            at = pl.ds(pl.multiple_of(f * (FF // shards) + j * 2 * LANES, LANES), 2 * LANES)
            yield pltpu.make_async_copy(up_s.at[slot, f], up_ref.at[:, at], sem.at[slot, 3 + f])

    @pl.when(j >= 2)
    def _():
        for copy in copies(j - 2):
            copy.wait()

    for f in range(shards):
        for i in range(2):
            up_s[slot, f, :, i * LANES : (i + 1) * LANES] = up_in[i, :, f * LANES : (f + 1) * LANES].astype(F32)
    one, two = qk_in[0].astype(F32), qk_in[1].astype(F32)
    qkv_s[slot, 0] = jnp.where(low, one, pltpu.roll(two, HDIM, 1))
    qkv_s[slot, 1] = jnp.where(low, pltpu.roll(one, HDIM, 1), two)
    for m in range(D // LANES):
        one = v_in[0, BIAS_ROWS:, m * LANES : (m + 1) * LANES].astype(F32)
        two = v_in[1, BIAS_ROWS:, m * LANES : (m + 1) * LANES].astype(F32)
        at = 2 * m * v_rows
        qkv_s[slot, 2, at : at + v_rows] = jnp.where(v_low, one, pltpu.roll(two, HDIM, 1))
        qkv_s[slot, 2, at + v_rows : at + 2 * v_rows] = jnp.where(v_low, pltpu.roll(one, HDIM, 1), two)
    for copy in copies(j):
        copy.start()
    for i in range(2):
        down_ref[i * LANES : (i + 1) * LANES] = rows_in[i, :LANES].astype(F32)
    out_ref[...] = head_in[0].astype(F32)

    @pl.when(j == steps - 1)
    def _():
        for copy in copies(j - 1):
            copy.wait()
        for copy in copies(j):
            copy.wait()


def place_grads(first, up, rows, heads, qk, v, shards):
    count, owned, units = up.shape
    part = units // shards
    pair = lambda array: pl.BlockSpec((2,) + array.shape[1:], lambda j, first: (j, 0, 0))
    grid_spec = pltpu.PrefetchScalarGridSpec(
        num_scalar_prefetch=1,
        grid=(count // 2,),
        in_specs=[
            pair(up), pair(rows), pair(qk), pair(v),
            pl.BlockSpec((1, HDIM, D), lambda j, first: (first[0] + j, 0, 0)),
        ],
        out_specs=[
            ANY_SPEC,
            ANY_SPEC,
            pl.BlockSpec((2 * part, D), lambda j, first: (j, 0)),
            pl.BlockSpec((HDIM, D), lambda j, first: (j, 0)),
        ],
        scratch_shapes=[
            pltpu.VMEM((2, 3, owned, LANES), F32),
            pltpu.VMEM((2, shards, owned, 2 * LANES), F32),
            DMA((2, 3 + shards)),
        ],
    )
    return pl.pallas_call(
        place_kernel,
        grid_spec=grid_spec,
        out_shape=[
            jax.ShapeDtypeStruct((owned, 3 * D), F32),
            jax.ShapeDtypeStruct((owned, FF), F32),
            jax.ShapeDtypeStruct((FF // shards, D), F32),
            jax.ShapeDtypeStruct((owned, D), F32),
        ],
        name="place_grads",
    )(first, up, rows, qk, v, heads)


def place_plain(first, a, b, shards):
    count, owned = a.shape[:2]
    part = FF // count // shards
    repeat = count // HEADS
    by_head = a.reshape(HEADS, repeat, owned, -1)[:, 0]
    qk_grad = by_head[:, :, :LANES].reshape(HEADS, owned, 2, HDIM)
    qk_grad = jnp.transpose(qk_grad, (1, 2, 0, 3)).reshape(owned, 2 * D)
    out_by_head = b.reshape(HEADS, repeat, b.shape[1], D)[:, 0]
    at_v = part + HDIM + BIAS_ROWS
    v_grad = out_by_head[:, at_v:].reshape(HEADS, -1, D // HDIM, HDIM)
    v_grad = jnp.transpose(v_grad, (2, 1, 0, 3)).reshape(owned, D)
    w_qkv_grad = jnp.concatenate([qk_grad, v_grad], axis=1).astype(F32)
    up_grad = a[:, :, LANES:].reshape(count, owned, shards, part)
    w_up_grad = jnp.transpose(up_grad, (1, 2, 0, 3)).reshape(owned, FF).astype(F32)
    w_down_grad = b[:, :part].reshape(FF // shards, D).astype(F32)
    out_grad = lax.dynamic_slice_in_dim(out_by_head[:, part : part + HDIM], first[0], HEADS // shards, axis=0)
    return w_qkv_grad, w_up_grad, w_down_grad, out_grad.reshape(owned, D).astype(F32)


def block_order(table, seg_ids):
    blocks = table.shape[0]
    segment = seg_ids.reshape(blocks, -1)[:, 0]
    number = jnp.arange(blocks, dtype=jnp.int32)
    stored = jnp.sum(jnp.where(table[:, None] == number[None, :], segment[None, :], 0), axis=1)
    key = stored * blocks + table
    rank = jnp.sum((key[None, :] < key[:, None]).astype(jnp.int32), axis=1)
    return jnp.sum(jnp.where(rank[None, :] == number[:, None], number[None, :], 0), axis=1), rank


def rotary_angles(table, positions):
    blocks = table.shape[0]
    by_block = positions.reshape(blocks, -1)
    number = jnp.arange(blocks, dtype=jnp.int32)
    pick = (table[:, None] == number[None, :])[:, :, None]
    place = jnp.sum(jnp.where(pick, by_block[None], 0), axis=1).reshape(1, -1)
    frequency = 10000.0 ** (-jnp.arange(0, ROT, 2, dtype=F32) / ROT)
    angle = frequency[:, None] * place.astype(F32)
    pair = jnp.concatenate([jnp.cos(angle), jnp.sin(angle)], axis=0)
    half = ROT // 2
    spread = np.zeros((ROT + 8, LANES), np.float32)
    for m in range(half):
        spread[m, m] = spread[m, m + half] = 1.0
        spread[half + m, HDIM + m], spread[half + m, HDIM + m + half] = -1.0, 1.0
    spread[ROT, ROT:HDIM] = 1.0
    return pair, jnp.asarray(spread)


def local(
    tokens, cotangent, w_qkv, w_up, w_out, w_down, b_qkv, b_up, b_out, b_down, ln_gain, ln_bias, block_table, seg_ids, positions,
):
    shards = lax.axis_size("fsdp")
    count = lax.axis_size("ctx")
    me = lax.axis_index("ctx")
    mine = lax.axis_index("fsdp")
    repeat = count // HEADS
    head = me // repeat
    owned = D // shards
    part = FF // count // shards
    units = part * shards
    heads_owned = HEADS // shards

    def columns(array, start, size):
        return lax.dynamic_slice_in_dim(array, start, size, axis=array.ndim - 1)

    def unit_columns(array):
        return [columns(array, f * (FF // shards) + part * me, part) for f in range(shards)]

    def head_columns(array):
        return [columns(array, k * D + HDIM * head, HDIM) for k in range(3)]

    whole_lanes = part == LANES and count == HEADS and heads_owned == count // 2
    if whole_lanes:
        vectors = (b_qkv, b_up, ln_gain, ln_bias, b_out, b_down)
        normed, slice_in, slice_out, bias, unit_bias, gains = prepare(
            tokens[0], vectors, w_qkv, w_up, w_down, w_out, count, shards
        )
    else:
        pad = jnp.zeros((owned, LANES - HDIM), BF16)
        slice_in = jnp.concatenate(head_columns(w_qkv) + [pad] + unit_columns(w_up), axis=1)
        slice_out = jnp.concatenate(
            [
                lax.dynamic_slice_in_dim(w_down, part * me, part, axis=0),
                lax.dynamic_slice_in_dim(w_out, HDIM * (head % heads_owned), HDIM, axis=0),
            ],
            axis=0,
        )
        bias = jnp.concatenate(head_columns(b_qkv.astype(F32)) + [jnp.ones((LANES - HDIM,), F32)])[None]
        unit_bias = jnp.concatenate(unit_columns(b_up.astype(F32)))[None]
        gain, out_bias = ln_gain.astype(F32)[None], (b_out.astype(F32) + b_down.astype(F32))[None]
        normed = norm(tokens[0], gain, ln_bias.astype(F32)[None])
    order, rank = block_order(block_table[0], seg_ids[0])
    pair, spread = rotary_angles(block_table[0], positions[0])
    first = (mine * heads_owned).astype(jnp.int32)[None]

    gathered, all_in, all_out, qkv, trig = first_stage(normed, slice_in, slice_out, bias, pair, spread, count, shards)
    w_in = all_in.reshape(D, 2 * LANES + units)
    if whole_lanes:
        output, merged, grad_up, g_up, g_down, g_head, up_sum, cot_sum, _ = core_stage(
            order, rank, qkv, cotangent[0], gathered, w_in, all_out, unit_bias, trig, tokens[0], gains, count, shards
        )
        input_grad, got_up, got_down, got_head, got_qk, got_v, small = end_stage(
            rank, merged, grad_up, w_in, gathered, g_up, g_down, g_head, up_sum, cot_sum,
            tokens[0], cotangent[0], gains, count, shards,
        )
        w_qkv_grad, w_up_grad, w_down_grad, w_out_grad = place_grads(first, got_up, got_down, got_head, got_qk, got_v, shards)
        bias_rows = got_v[:, :4].astype(F32)
    else:
        partial, grad_up, scaled, g_out, g_up, up_sum, cot_sum = middle_stage(
            order, rank, qkv, cotangent[0], gathered, w_in, all_out, unit_bias, count, shards
        )
        output, merged = slopes_stage(order, partial, qkv, scaled, trig, tokens[0], out_bias, count)
        if repeat > 1:
            merged = jnp.where(me % repeat == 0, merged, jnp.zeros_like(merged))
        input_grad, got_in, got_out, small = last_stage(
            rank, merged, grad_up, w_in, gathered, g_out, g_up, up_sum, cot_sum, tokens[0], cotangent[0], gain, count, shards
        )
        w_qkv_grad, w_up_grad, w_down_grad, w_out_grad = place_plain(first, got_in, got_out, shards)
        at_bias = part + HDIM
        bias_rows = got_out[:, at_bias : at_bias + 4].astype(F32)

    sums = bias_rows[:, :2] + bias_rows[:, 2:]
    head_sums = sums[:, 0].reshape(HEADS, repeat, D)[:, 0, : 3 * HDIM].reshape(HEADS, 3, HDIM)
    b_qkv_grad = jnp.swapaxes(head_sums, 0, 1).reshape(3 * D)
    b_up_grad = jnp.transpose(
        sums[:, 0, 2 * LANES : 2 * LANES + units].reshape(count, shards, part), (1, 0, 2)
    ).reshape(FF)
    b_out_grad = sums[0, 1]
    return (
        output[None], input_grad[None], w_qkv_grad, w_up_grad, w_out_grad, w_down_grad,
        b_qkv_grad, b_up_grad, b_out_grad, b_out_grad, small[0], small[1],
    )


def solution(mesh):
    rows = P("fsdp", None)
    in_specs = (P("fsdp", "ctx", None),) * 2 + (rows,) * 4 + (P(),) * 6 + (rows,) * 3
    out_specs = (P("fsdp", "ctx", None),) * 2 + (rows,) * 4 + (P(),) * 6
    return jax.shard_map(local, mesh=mesh, in_specs=in_specs, out_specs=out_specs, check_vma=False)
```
